32 devices in a mesh: boxes: 32 (over z, y, x, core).
Axes of the slice: x: 2, y: 2, z: 4, core: 2. Of those that a mesh axis runs over, the one named last changes fastest.
Arguments:
- random_block: bfloat16 [512, 256, 128], P('boxes'), may hold values from -6 to 6
- sample_block: bfloat16 [512, 256, 128], P('boxes'), may hold values from -12 to 12
- near_blocks: bfloat16 [512, 8, 256, 256], P('boxes'), may hold values from -0.375 to 0.375
- near_index: int32 [512, 8], P('boxes'), may hold values from 0 to 511, as said below
- near_count: int32 [512], P('boxes'), may hold values from 2 to 8
Outputs:
- leaf_sketch: bfloat16 [512, 256, 128], P('boxes')
- level_sketch: bfloat16 [32, 9, 128, 128], P('boxes')
The draws below stay inside these ranges and needn't reach their ends.
Inputs may be any that keep to these rules, and one draw needn't show every extreme that they name: near_index[b, 0] = b; every entry lies within 16 boxes of b; entries at slots from near_count[b] on are ignored.
All inputs are finite; a program needn't handle non-finite values.
Results may differ from the reference program's by a relative error of at most 0.001.
Values may be sent and summed in bfloat16 or wider, within the bound.
A program may use at most 192 MiB of HBM per device.

```python
import jax
import jax.numpy as jnp
from jax import lax

LEAF = 256
RANK = 64
SAMPLES = 128
MAXNEAR = 8
BOX_DEV = 16
NBOX = 512
LEVELS = 9
N_BOXES = 32


def draw_near_count(key, part):
    heavy_flag = jax.random.randint(jax.random.fold_in(key, 12), (NBOX // BOX_DEV,), 0, 2)
    heavy_rows = jnp.repeat(heavy_flag, BOX_DEV)
    light_draw = jax.random.randint(jax.random.fold_in(key, 13), (NBOX,), 2, MAXNEAR // 2 + 1)
    heavy_draw = jax.random.randint(jax.random.fold_in(key, 14), (NBOX,), MAXNEAR // 2 + 1, MAXNEAR + 1)
    counts = jnp.where(heavy_rows == 1, heavy_draw, light_draw)
    return counts.at[0].set(MAXNEAR).astype(jnp.int32)


def draw_near_index(key, part):
    boxes_ids = jnp.arange(NBOX)
    offsets = jax.random.randint(jax.random.fold_in(key, 21), (NBOX, MAXNEAR), -BOX_DEV, BOX_DEV + 1)
    sign_pick = jax.random.randint(jax.random.fold_in(key, 22), (NBOX,), 0, 2) * 2 - 1
    offsets = offsets.at[:, 0].set(0).at[:, 1].set(sign_pick * BOX_DEV)
    return jnp.clip(boxes_ids[:, None] + offsets, 0, NBOX - 1).astype(jnp.int32)


def steps_of(stream_key, extent, pieces, smallest, top_value):
    level, own = 1.0, jax.random.fold_in(stream_key, 6)
    for position, parts in pieces:
        draws = jnp.exp(jax.random.uniform(jax.random.fold_in(own, position), (parts,), jnp.float32, smallest / len(pieces), top_value / len(pieces)))
        level = level * jnp.repeat(draws, extent[position] // parts).reshape([-1 if axis == position else 1 for axis in range(len(extent))])
    return level


def scatter_about(rng, dims, scale, most, cuts=(), dtype=jnp.bfloat16):
    gain = steps_of(rng, dims, cuts, -0.22, 0.18) if cuts else 1.0
    array = jax.random.normal(rng, dims, jnp.float32) * scale * gain
    return jnp.minimum(jnp.maximum(array, -most), most).astype(dtype)


def setup_inputs(seed: int = 0) -> dict:
    arg_keys = jax.random.split(jax.random.key(seed), 6)
    return {
        "random_block": scatter_about(arg_keys[0], (NBOX, LEAF, SAMPLES), 1.0, 6.0, ((0, 32),)),
        "sample_block": scatter_about(arg_keys[1], (NBOX, LEAF, SAMPLES), 2.0, 12.0, ((0, 32),)),
        "near_blocks": scatter_about(arg_keys[2], (NBOX, MAXNEAR, LEAF, LEAF), LEAF ** -0.5, 0.375, ((0, 32),)),
        "near_index": draw_near_index(jax.random.fold_in(arg_keys[5], 71), 0),
        "near_count": draw_near_count(jax.random.fold_in(arg_keys[5], 71), 0),
    }


exact_mode = lax.Precision.HIGHEST

def lower_solve(factor, compact):
    return jax.scipy.linalg.solve_triangular(factor, compact.T, lower=True)

def basis_step(sample, random):
    compact = sample[:, :, :RANK] + sample[:, :, RANK:]
    gram = jnp.einsum('bik,bil->bkl', compact, compact, precision=exact_mode)
    factor = jnp.linalg.cholesky(gram)
    rows_q = jax.vmap(lower_solve)(factor, compact)
    reduced = jnp.einsum('bki,bis->bks', rows_q, sample, precision=exact_mode)
    projected = jnp.einsum('bki,bis->bks', rows_q, random, precision=exact_mode)
    sketch = jnp.einsum('bki,bks->bis', rows_q, projected, precision=exact_mode)
    return (reduced, projected, sketch)

def reference(random_block, sample_block, near_blocks, near_index, near_count):
    slots = jnp.arange(MAXNEAR)

    def near_term(packed):
        blocks, indices, length = packed
        picked = jnp.take(random_block, indices, axis=0).astype(jnp.float32)
        keep_mask = (slots < length).astype(jnp.float32)
        picked = picked * keep_mask[:, None, None]
        return jnp.einsum('mij,mjs->is', blocks.astype(jnp.float32), picked)
    near_sum = lax.map(near_term, (near_blocks, near_index, near_count))
    far_sample = sample_block.astype(jnp.float32) - near_sum
    reduced, projected, sketch = basis_step(far_sample, random_block.astype(jnp.float32))
    leaf_sketch = sketch.astype(jnp.bfloat16)
    firsts = jnp.arange(N_BOXES) * BOX_DEV
    records = []
    nodes = NBOX
    for height in range(LEVELS):
        nodes = nodes // 2
        reduced, projected, sketch = basis_step(reduced.reshape(nodes, 2 * RANK, SAMPLES), projected.reshape(nodes, 2 * RANK, SAMPLES))
        records.append(jnp.take(sketch, firsts // 2 ** (height + 1), axis=0))
    level_sketch = jnp.stack(records, axis=1).astype(jnp.bfloat16)
    return (leaf_sketch, level_sketch)
```

```python
import functools

import jax
import jax.numpy as jnp
from jax import lax
from jax.experimental import pallas as pl
from jax.experimental.pallas import tpu as pltpu
from jax.sharding import PartitionSpec as P

AXIS = "boxes"
MESH = pl.DeviceIdType.MESH


def fine_dot(a, b, dims=((1,), (0,))):
    return lax.dot_general(
        a, b, (dims, ((), ())), precision=lax.Precision.HIGH, preferred_element_type=jnp.float32
    )


def halo_kernel(index, counts, source, blocks, sample, part, halo, wide, copy_sem, sent, landed):
    box = pl.program_id(0)
    count = source.shape[0]
    slots, samples = blocks.shape[1], sample.shape[2]
    size = lax.axis_size(AXIS)
    me = lax.axis_index(AXIS)
    core = lax.rem(me, 2)
    partner = me + 1 - 2 * core
    across = me - 1 + 2 * core
    inside = (across >= 0) & (across < size)

    def local_copy():
        return pltpu.make_async_copy(source, wide.at[pl.ds(0, count)], copy_sem)

    def near_copy():
        return pltpu.make_async_remote_copy(
            src_ref=source,
            dst_ref=wide.at[pl.ds(count, count)],
            send_sem=sent.at[0],
            recv_sem=landed.at[0],
            device_id=(partner,),
            device_id_type=MESH,
        )

    def far_copy():
        return pltpu.make_async_remote_copy(
            src_ref=source,
            dst_ref=halo,
            send_sem=sent.at[1],
            recv_sem=landed.at[1],
            device_id=(across,),
            device_id_type=MESH,
        )

    @pl.when(box == 0)
    def _():
        local_copy().start()
        barrier = pltpu.get_barrier_semaphore()
        pl.semaphore_signal(barrier, inc=1, device_id=(partner,), device_id_type=MESH)

        @pl.when(inside)
        def _():
            pl.semaphore_signal(barrier, inc=1, device_id=(across,), device_id_type=MESH)
            pl.semaphore_wait(barrier, 2)
            far_copy().start()

        @pl.when(jnp.logical_not(inside))
        def _():
            pl.semaphore_wait(barrier, 1)

        near_copy().start()
        local_copy().wait()
        near_copy().wait()

    total = jnp.zeros(sample.shape[1:], jnp.float32)
    for slot in range(slots):
        place = index[box, slot] - me * count
        other = place - (1 - 2 * core) * count
        own = (place >= 0) & (place < count)
        beside = (other >= 0) & (other < count)
        pick = jnp.where(own, place, jnp.where(beside, other + count, 0))
        keep = ((own | beside) & (slot < counts[box])).astype(jnp.float32).astype(jnp.bfloat16)
        total += jnp.dot(blocks[0, slot], wide[pick] * keep, preferred_element_type=jnp.float32)
    part[0] = sample[0].astype(jnp.float32) - total

    @pl.when((box == pl.num_programs(0) - 1) & inside)
    def _():
        far_copy().wait()


def halo_call(index, counts, source, blocks, sample):
    count, rows, samples = sample.shape
    slots = blocks.shape[1]
    anywhere = pl.BlockSpec(memory_space=pl.ANY)
    return pl.pallas_call(
        halo_kernel,
        grid_spec=pltpu.PrefetchScalarGridSpec(
            num_scalar_prefetch=0,
            grid=(count,),
            in_specs=[
                pl.BlockSpec(memory_space=pltpu.SMEM),
                pl.BlockSpec(memory_space=pltpu.SMEM),
                anywhere,
                pl.BlockSpec((1, slots, rows, rows), lambda b: (b, 0, 0, 0)),
                pl.BlockSpec((1, rows, samples), lambda b: (b, 0, 0)),
            ],
            out_specs=[pl.BlockSpec((1, rows, samples), lambda b: (b, 0, 0)), anywhere],
            scratch_shapes=[
                pltpu.VMEM((2 * count, rows, samples), jnp.bfloat16),
                pltpu.SemaphoreType.DMA,
                pltpu.SemaphoreType.DMA((2,)),
                pltpu.SemaphoreType.DMA((2,)),
            ],
        ),
        out_shape=[
            jax.ShapeDtypeStruct(sample.shape, jnp.float32),
            jax.ShapeDtypeStruct(sample.shape, jnp.bfloat16),
        ],
        compiler_params=pltpu.CompilerParams(collective_id=0, has_side_effects=True),
        name="halo",
    )(index, counts, source, blocks, sample)


def split_three(value):
    high = value.astype(jnp.bfloat16)
    rest = value - high.astype(jnp.float32)
    middle = rest.astype(jnp.bfloat16)
    low = (rest - middle.astype(jnp.float32)).astype(jnp.bfloat16)
    return high, middle, low


def gram_kernel(index, counts, part, source, halo, blocks, start, moment, compact, held, far, sems):
    step = pl.program_id(0)
    steps = pl.num_programs(0)
    together, rows, samples = part.shape
    count = halo.shape[0]
    slots = held.shape[1]
    half = samples // 2
    me = lax.axis_index(AXIS)
    core = lax.rem(me, 2)
    base = (me - 1 + 2 * core) * count

    def wanted(box, slot):
        place = index[box, slot] - base
        return place, (place >= 0) & (place < count) & (slot < counts[box])

    def fetch(box, slot):
        return pltpu.make_async_copy(blocks.at[box, slot], held.at[box, slot], sems.at[box])

    def issue(which):
        for member in range(together):
            box = which * together + member
            for slot in range(1, slots):
                place, needed = wanted(box, slot)

                @pl.when(needed)
                def _():
                    fetch(box, slot).start()

    @pl.when(step == 0)
    def _():
        issue(0)

    @pl.when(step + 1 < steps)
    def _():
        issue(step + 1)

    for member in range(together):
        box = step * together + member
        far[member] = part[member]
        for slot in range(1, slots):
            place, needed = wanted(box, slot)

            @pl.when(needed)
            def _():
                fetch(box, slot).wait()

        for slot in range(1, slots):
            place, needed = wanted(box, slot)

            @pl.when(needed)
            def _():
                far[member] -= jnp.dot(
                    held[box, slot], halo[place], preferred_element_type=jnp.float32
                )

    lanes_rows = lax.broadcasted_iota(jnp.int32, (rows, samples), 1)
    lanes = lax.broadcasted_iota(jnp.int32, (half, samples), 1)
    diagonal = lanes - half == lax.broadcasted_iota(jnp.int32, (half, samples), 0)
    for member in range(together):
        value = far[member]
        doubled = value + pltpu.roll(value, half, 1)
        flipped = doubled.T[:half]
        high, middle, low = split_three(flipped)
        left = jnp.concatenate([high, middle, low], axis=0)
        top = doubled.astype(jnp.bfloat16)
        next_top = doubled - top.astype(jnp.float32)
        both = jnp.where(lanes_rows < half, top.astype(jnp.float32), next_top).astype(jnp.bfloat16)
        compact[member] = both
        product = jnp.dot(
            left,
            jnp.concatenate([source[member], both], axis=1),
            preferred_element_type=jnp.float32,
        )
        moment[member] = product[:half, :samples] + (
            product[half : 2 * half, :samples] + product[2 * half :, :samples]
        )
        first = product[:half, samples:]
        second = product[half : 2 * half, samples:]
        third = product[2 * half :, samples:]
        turned = jnp.concatenate([third, jnp.zeros_like(third)], axis=0).T[:half]
        small = second + third + turned
        shifted = pltpu.roll(first + second, half, 1)
        start[member] = jnp.where(
            lanes < half, first + (shifted + small), diagonal.astype(jnp.float32)
        )


def gram_call(index, counts, part, source, halo, blocks):
    count, rows, samples = part.shape
    slots = blocks.shape[1]
    half = samples // 2
    together = 4 if count % 4 == 0 else 1
    anywhere = pl.BlockSpec(memory_space=pl.ANY)
    smem = pl.BlockSpec(memory_space=pltpu.SMEM)

    def per_step(*tail):
        return pl.BlockSpec((together, *tail), lambda b: (b, *(0 for _ in tail)))

    return pl.pallas_call(
        gram_kernel,
        grid=(count // together,),
        in_specs=[
            smem,
            smem,
            per_step(rows, samples),
            per_step(rows, samples),
            pl.BlockSpec((count, rows, samples), lambda b: (0, 0, 0)),
            anywhere,
        ],
        out_specs=[per_step(half, samples), per_step(half, samples), per_step(rows, samples)],
        out_shape=[
            jax.ShapeDtypeStruct((count, half, samples), jnp.float32),
            jax.ShapeDtypeStruct((count, half, samples), jnp.float32),
            jax.ShapeDtypeStruct((count, rows, samples), jnp.bfloat16),
        ],
        scratch_shapes=[
            pltpu.VMEM((count, slots, rows, rows), jnp.bfloat16),
            pltpu.VMEM((together, rows, samples), jnp.float32),
            pltpu.SemaphoreType.DMA((count,)),
        ],
        name="gram",
    )(index, counts, part, source, halo, blocks)


def factor(work, first, nodes, low, high, width):
    half, samples = work.shape[1:]
    octets = half // 8
    row8 = lax.broadcasted_iota(jnp.int32, (nodes, 8, samples), 1)

    def spread_row(value, row):
        return jnp.broadcast_to(value[:, row : row + 1, :], value.shape)

    def spread_column(value, lane):
        return jnp.broadcast_to(value[:, :, lane : lane + 1], value.shape)

    def octet(place):
        return work[first : first + nodes, 8 * place : 8 * place + 8, :]

    def put(place, value):
        work[first : first + nodes, 8 * place : 8 * place + 8, :] = value

    for place in range(low, high):
        base = 8 * place
        head = octet(place)
        upper, pivots = head, None
        for begin in range(0, 8, width):
            rows = range(begin, begin + width)
            columns = {row: spread_column(head, base + row) for row in rows}
            for row in rows:
                pivot = spread_row(columns[row], row)
                pivots = pivot if pivots is None else jnp.where(row8 == row, pivot, pivots)
                scaled = jnp.where(row8 == row, 0.0, columns[row] * (1.0 / pivot))
                line = spread_row(head, row)
                if row:
                    upper = jnp.where(row8 == row, line, upper)
                head = head - scaled * line
                for later in range(row + 1, begin + width):
                    columns[later] = columns[later] - scaled * spread_row(columns[later], row)
        put(place, upper * lax.rsqrt(pivots))
        if place + 1 == octets:
            break
        head = head * (1.0 / pivots)
        lines = [spread_row(head, row) for row in range(8)]
        for other in range(place + 1, octets):
            value = octet(other)
            columns = [spread_column(value, base + row) for row in range(8)]
            for row in range(8):
                value = value - columns[row] * lines[row]
            put(other, value)


def packed(gram, moment):
    rows = gram.shape[0] // 2
    half = gram.shape[1] // 2
    lanes = lax.broadcasted_iota(jnp.int32, (rows, 2 * half), 1)
    top = jnp.where(lanes < half, gram[:rows], pltpu.roll(gram[rows:], half, 1))
    return jnp.concatenate([top, moment], axis=0)


def unpacked(value, half):
    rows = half // 2
    lanes = lax.broadcasted_iota(jnp.int32, (half, 2 * half), 1)
    diagonal = lanes - half == lax.broadcasted_iota(jnp.int32, (half, 2 * half), 0)
    gram = jnp.concatenate([value[:rows], pltpu.roll(value[:rows], half, 1)], axis=0)
    return jnp.where(lanes < half, gram, diagonal.astype(jnp.float32))


def tree_kernel(spread, start, moment, work, local, sums, arrived, sent, landed):
    count, half, samples = start.shape
    depth = count.bit_length() - 1
    me = lax.axis_index(AXIS)
    bits = [lax.rem(lax.div(me, 1 << step), 2) for step in range(spread)]
    partners = [me + (1 - 2 * bit) * (1 << step) for step, bit in enumerate(bits)]
    barrier = pltpu.get_barrier_semaphore()
    for partner in partners:
        pl.semaphore_signal(barrier, inc=1, device_id=(partner,), device_id_type=MESH)

    def exchange(step):
        return pltpu.make_async_remote_copy(
            src_ref=sums.at[step],
            dst_ref=arrived.at[step],
            send_sem=sent.at[step],
            recv_sem=landed.at[step],
            device_id=(partners[step],),
            device_id_type=MESH,
        )

    grams = {(0, leaf): start[leaf] for leaf in range(count)}
    moments = {(0, leaf): moment[leaf] for leaf in range(count)}
    for height in range(1, depth + 1):
        for node in range(count >> height):
            for table in (grams, moments):
                table[height, node] = (
                    table[height - 1, 2 * node] + table[height - 1, 2 * node + 1]
                )
    sums[0] = packed(grams[depth, 0], moments[depth, 0])
    pl.semaphore_wait(barrier, spread)
    copies = [exchange(step) for step in range(spread)]
    copies[0].start()

    lanes = lax.broadcasted_iota(jnp.int32, (half, samples), 1)
    diagonal = lanes - half == lax.broadcasted_iota(jnp.int32, (half, samples), 0)
    for leaf in range(count):
        work[leaf] = start[leaf]
    place = count
    for height in range(1, depth + 1):
        local[height - 1] = moments[height, 0]
        for side in range(1 if height == depth else 2):
            work[place] = jnp.where(
                lanes < half, grams[height, side], diagonal.astype(jnp.float32)
            )
            place += 1
    octets = half // 8
    for step in range(spread):
        factor(
            work, 0, place, octets * step // spread, octets * (step + 1) // spread, 4
        )
        copies[step].wait()
        sums[step + 1] = sums[step] + arrived[step]
        if step + 1 < spread:
            copies[step + 1].start()


def tree_call(start, moment, spread):
    count, half, samples = start.shape
    depth = count.bit_length() - 1
    nodes = count + 2 * depth - 1
    rows = half // 2 + half
    vmem = pl.BlockSpec(memory_space=pltpu.VMEM)
    return pl.pallas_call(
        functools.partial(tree_kernel, spread),
        in_specs=[vmem] * 2,
        out_specs=[vmem] * 4,
        out_shape=[
            jax.ShapeDtypeStruct((nodes, half, samples), jnp.float32),
            jax.ShapeDtypeStruct((depth, half, samples), jnp.float32),
            jax.ShapeDtypeStruct((spread + 1, rows, samples), jnp.float32),
            jax.ShapeDtypeStruct((spread, rows, samples), jnp.float32),
        ],
        scratch_shapes=[
            pltpu.SemaphoreType.DMA((spread,)),
            pltpu.SemaphoreType.DMA((spread,)),
        ],
        compiler_params=pltpu.CompilerParams(collective_id=1, has_side_effects=True),
        name="tree",
    )(start, moment)


def out_kernel(work, moment, local, sums, arrived, compact, leaf_out, level_out, tops):
    count, half, samples = moment.shape
    depth = count.bit_length() - 1
    spread = arrived.shape[0]
    me = lax.axis_index(AXIS)
    lanes = lax.broadcasted_iota(jnp.int32, (half, samples), 1)
    triangle = lanes >= lax.broadcasted_iota(jnp.int32, (half, samples), 0)
    corner = triangle & (lanes < half)
    blank = jnp.zeros((half, samples), jnp.float32)

    def solved(matrix, right):
        middle = fine_dot(matrix, jnp.concatenate([blank, right], axis=0))
        return fine_dot(matrix, middle, ((0,), (0,)))[half:]

    def sketch(one, two, answer):
        stacked = jnp.concatenate(
            [jnp.where(corner, one, 0.0), jnp.where(corner, two, 0.0)], axis=0
        )
        return fine_dot(stacked, jnp.concatenate([answer, blank], axis=0))

    for step in range(spread):
        tops[2 * step] = unpacked(arrived[step], half)
        tops[2 * step + 1] = unpacked(sums[step + 1], half)
    factor(tops, 0, 2 * spread, 0, half // 8, 8)

    for leaf in range(count):
        answer = solved(work[leaf], moment[leaf])
        high = answer.astype(jnp.bfloat16)
        low = (answer - high.astype(jnp.float32)).astype(jnp.bfloat16)
        pair = jnp.concatenate([high, low], axis=1)
        both = jnp.dot(
            compact[leaf],
            jnp.concatenate([pair, pair], axis=0),
            preferred_element_type=jnp.float32,
        )
        leaf_out[leaf] = (both[:, :samples] + both[:, samples:]).astype(leaf_out.dtype)
    for height in range(1, depth + 1):
        first = 0 if height == 1 else count + 2 * (height - 2)
        answer = solved(work[count + 2 * (height - 1)], local[height - 1])
        level_out[0, height - 1] = sketch(work[first], work[first + 1], answer).astype(
            level_out.dtype
        )
    for step in range(spread):
        mine = work[count + 2 * (depth - 1)] if step == 0 else tops[2 * step - 1]
        other = tops[2 * step]
        odd = lax.rem(lax.div(me, 1 << step), 2) == 1
        answer = solved(tops[2 * step + 1], sums[step + 1, half // 2 :, :])
        level_out[0, depth + step] = sketch(
            jnp.where(odd, other, mine), jnp.where(odd, mine, other), answer
        ).astype(level_out.dtype)


def out_call(work, moment, local, sums, arrived, compact):
    count, rows, samples = compact.shape
    half = moment.shape[1]
    spread = arrived.shape[0]
    depth = count.bit_length() - 1
    vmem = pl.BlockSpec(memory_space=pltpu.VMEM)
    return pl.pallas_call(
        out_kernel,
        in_specs=[vmem] * 6,
        out_specs=[vmem] * 2,
        out_shape=[
            jax.ShapeDtypeStruct((count, rows, samples), jnp.bfloat16),
            jax.ShapeDtypeStruct((1, depth + spread, samples, samples), jnp.bfloat16),
        ],
        scratch_shapes=[pltpu.VMEM((2 * spread, half, samples), jnp.float32)],
        name="out",
    )(work, moment, local, sums, arrived, compact)


def per_device(random_block, sample_block, near_blocks, near_index, near_count):
    spread = lax.axis_size(AXIS).bit_length() - 1
    part, halo = halo_call(near_index, near_count, random_block, near_blocks, sample_block)
    start, moment, compact = gram_call(
        near_index, near_count, part, random_block, halo, near_blocks
    )
    work, local, sums, arrived = tree_call(start, moment, spread)
    return tuple(out_call(work, moment, local, sums, arrived, compact))


def solution(mesh):
    return jax.shard_map(
        per_device,
        mesh=mesh,
        in_specs=(
            P(AXIS, None, None),
            P(AXIS, None, None),
            P(AXIS, None, None, None),
            P(AXIS, None),
            P(AXIS),
        ),
        out_specs=(P(AXIS, None, None), P(AXIS, None, None, None)),
        check_vma=False,
    )
```

```python
import functools

import jax
import jax.numpy as jnp
from jax import lax
from jax.experimental import pallas as pl
from jax.experimental.pallas import tpu as pltpu
from jax.sharding import PartitionSpec as P

AXIS = "boxes"
MESH = pl.DeviceIdType.MESH


def fine_dot(a, b, dims=((1,), (0,))):
    return lax.dot_general(
        a, b, (dims, ((), ())), precision=lax.Precision.HIGH, preferred_element_type=jnp.float32
    )


def halo_kernel(
    index, counts, source, blocks, sample, part, halo, held, wide, base, loads, arrivals, sent, landed
):
    count, slots, rows = held.shape[:3]
    samples = part.shape[2]
    size = lax.axis_size(AXIS)
    me = lax.axis_index(AXIS)
    core = lax.rem(me, 2)
    partner = me + 1 - 2 * core
    across = me - 1 + 2 * core
    inside = (across >= 0) & (across < size)
    near_copy = pltpu.make_async_remote_copy(
        src_ref=source,
        dst_ref=wide.at[pl.ds(count, count)],
        send_sem=sent.at[0],
        recv_sem=landed.at[0],
        device_id=(partner,),
        device_id_type=MESH,
    )
    far_copy = pltpu.make_async_remote_copy(
        src_ref=source,
        dst_ref=halo,
        send_sem=sent.at[1],
        recv_sem=landed.at[1],
        device_id=(across,),
        device_id_type=MESH,
    )
    own_copy = pltpu.make_async_copy(source, wide.at[pl.ds(0, count)], loads.at[0])
    sample_copy = pltpu.make_async_copy(sample, base, loads.at[1])

    def fetch(box):
        return pltpu.make_async_copy(blocks.at[box], held.at[box], arrivals.at[box])

    barrier = pltpu.get_barrier_semaphore()
    pl.semaphore_signal(barrier, inc=1, device_id=(partner,), device_id_type=MESH)

    @pl.when(inside)
    def _():
        pl.semaphore_signal(barrier, inc=1, device_id=(across,), device_id_type=MESH)
        pl.semaphore_wait(barrier, 2)
        far_copy.start()

    @pl.when(jnp.logical_not(inside))
    def _():
        pl.semaphore_wait(barrier, 1)

    near_copy.start()
    own_copy.start()
    sample_copy.start()
    for box in range(count):
        fetch(box).start()
    own_copy.wait()
    sample_copy.wait()
    near_copy.wait()

    def near(box, carry):
        fetch(box).wait()
        picked = []
        for slot in range(slots):
            place = index[slot, box] - me * count
            other = place - (1 - 2 * core) * count
            own = (place >= 0) & (place < count)
            beside = (other >= 0) & (other < count)
            pick = jnp.where(own, place, jnp.where(beside, other + count, 0))
            keep = ((own | beside) & (slot < counts[box])).astype(jnp.float32)
            picked.append(wide[pick] * keep.astype(jnp.bfloat16))
        part[box] = base[box].astype(jnp.float32) - jnp.dot(
            jnp.concatenate([held[box, slot] for slot in range(slots)], axis=1),
            jnp.concatenate(picked, axis=0),
            preferred_element_type=jnp.float32,
        )
        return carry

    lax.fori_loop(0, count, near, 0)

    @pl.when(inside)
    def _():
        far_copy.wait()


def halo_call(index, counts, source, blocks, sample):
    count, rows, samples = sample.shape
    anywhere = pl.BlockSpec(memory_space=pl.ANY)
    smem = pl.BlockSpec(memory_space=pltpu.SMEM)
    vmem = pl.BlockSpec(memory_space=pltpu.VMEM)
    return pl.pallas_call(
        halo_kernel,
        in_specs=[smem, smem, anywhere, anywhere, anywhere],
        out_specs=[vmem, anywhere, vmem],
        out_shape=[
            jax.ShapeDtypeStruct(sample.shape, jnp.float32),
            jax.ShapeDtypeStruct(sample.shape, jnp.bfloat16),
            jax.ShapeDtypeStruct(blocks.shape, jnp.bfloat16),
        ],
        scratch_shapes=[
            pltpu.VMEM((2 * count, rows, samples), jnp.bfloat16),
            pltpu.VMEM((count, rows, samples), jnp.bfloat16),
            pltpu.SemaphoreType.DMA((2,)),
            pltpu.SemaphoreType.DMA((count,)),
            pltpu.SemaphoreType.DMA((2,)),
            pltpu.SemaphoreType.DMA((2,)),
        ],
        compiler_params=pltpu.CompilerParams(
            collective_id=0, has_side_effects=True, vmem_limit_bytes=30 * 2**20
        ),
        name="halo",
    )(index, counts, source, blocks, sample)


def gram_kernel(
    index, counts, part, source, halo, blocks, start, moment, compact, far, picks
):
    count, rows, samples = far.shape
    slots = blocks.shape[1]
    half = samples // 2
    me = lax.axis_index(AXIS)
    core = lax.rem(me, 2)
    base = (me - 1 + 2 * core) * count

    found = jnp.int32(0)
    for box in range(count):
        far[box] = part[box]
        for slot in range(1, slots):
            place = index[slot, box] - base
            needed = (place >= 0) & (place < count) & (slot < counts[box])
            picks[found] = (box * slots + slot) * count + place
            found = found + needed.astype(jnp.int32)
    group = 4

    def multiply(turn, carry):
        terms = []
        for member in range(group):
            entry = turn * group + member
            code = picks[jnp.minimum(entry, found - 1)]
            block = lax.div(code, count)
            box = lax.div(block, slots)
            keep = (entry < found).astype(jnp.float32).astype(jnp.bfloat16)
            terms.append(
                (
                    box,
                    jnp.dot(
                        blocks[box, lax.rem(block, slots)],
                        halo[lax.rem(code, count)] * keep,
                        preferred_element_type=jnp.float32,
                    ),
                )
            )
        for box, term in terms:
            far[box] -= term
        return carry

    lax.fori_loop(0, lax.div(found + group - 1, group), multiply, 0)

    lanes_rows = lax.broadcasted_iota(jnp.int32, (rows, samples), 1)
    lanes = lax.broadcasted_iota(jnp.int32, (half, samples), 1)
    diagonal = lanes - half == lax.broadcasted_iota(jnp.int32, (half, samples), 0)
    together = 4 if count % 4 == 0 else 1

    def reduce(turn, carry):
        for member in range(together):
            box = turn * together + member
            value = far[box]
            doubled = value + pltpu.roll(value, half, 1)
            high = doubled.astype(jnp.bfloat16).astype(jnp.float32)
            both = jnp.where(lanes_rows < half, high, doubled - high).astype(jnp.bfloat16)
            compact[box] = both
            product = jnp.dot(
                both.T,
                jnp.concatenate([source[box], both], axis=1),
                preferred_element_type=jnp.float32,
            )
            moment[box] = product[:half, :samples] + product[half:, :samples]
            mixed = product[:half, samples:] + product[half:, samples:]
            start[box] = jnp.where(
                lanes < half, mixed + pltpu.roll(mixed, half, 1), diagonal.astype(jnp.float32)
            )
        return carry

    lax.fori_loop(0, count // together, reduce, 0)


def gram_call(index, counts, part, source, halo, blocks):
    count, rows, samples = part.shape
    slots = blocks.shape[1]
    half = samples // 2
    most = count * (slots - 1)
    smem = pl.BlockSpec(memory_space=pltpu.SMEM)
    vmem = pl.BlockSpec(memory_space=pltpu.VMEM)
    return pl.pallas_call(
        gram_kernel,
        in_specs=[smem, smem, vmem, vmem, vmem, vmem],
        out_specs=[vmem] * 3,
        out_shape=[
            jax.ShapeDtypeStruct((count, half, samples), jnp.float32),
            jax.ShapeDtypeStruct((count, half, samples), jnp.float32),
            jax.ShapeDtypeStruct((count, rows, samples), jnp.bfloat16),
        ],
        scratch_shapes=[
            pltpu.VMEM((count, rows, samples), jnp.float32),
            pltpu.SMEM((most + 1,), jnp.int32),
        ],
        compiler_params=pltpu.CompilerParams(vmem_limit_bytes=12 * 2**20),
        name="gram",
    )(index, counts, part, source, halo, blocks)


def factor(work, first, nodes, low, high, width):
    half, samples = work.shape[1:]
    octets = half // 8
    row8 = lax.broadcasted_iota(jnp.int32, (nodes, 8, samples), 1)

    def spread_row(value, row):
        return jnp.broadcast_to(value[:, row : row + 1, :], value.shape)

    def spread_column(value, lane):
        flat = value.reshape(nodes * 8, samples)
        return jnp.broadcast_to(flat[:, lane : lane + 1], flat.shape).reshape(value.shape)

    def octet(place):
        return work[first : first + nodes, 8 * place : 8 * place + 8, :]

    def put(place, value):
        work[first : first + nodes, 8 * place : 8 * place + 8, :] = value

    for place in range(low, high):
        base = 8 * place
        head = octet(place)
        upper, pivots = head, None
        for begin in range(0, 8, width):
            rows = range(begin, begin + width)
            columns = {row: spread_column(head, base + row) for row in rows}
            for row in rows:
                pivot = spread_row(columns[row], row)
                pivots = pivot if pivots is None else jnp.where(row8 == row, pivot, pivots)
                scaled = jnp.where(row8 == row, 0.0, columns[row] * (1.0 / pivot))
                line = spread_row(head, row)
                if row:
                    upper = jnp.where(row8 == row, line, upper)
                head = head - scaled * line
                for later in range(row + 1, begin + width):
                    columns[later] = columns[later] - scaled * spread_row(columns[later], row)
        put(place, upper * lax.rsqrt(pivots))
        if place + 1 == octets:
            break
        head = head * (1.0 / pivots)
        lines = [spread_row(head, row) for row in range(8)]
        for other in range(place + 1, octets):
            value = octet(other)
            columns = [spread_column(value, base + row) for row in range(8)]
            for row in range(8):
                value = value - columns[row] * lines[row]
            put(other, value)


def packed(gram, moment):
    rows = gram.shape[0] // 2
    half = gram.shape[1] // 2
    lanes = lax.broadcasted_iota(jnp.int32, (rows, 2 * half), 1)
    top = jnp.where(lanes < half, gram[:rows], pltpu.roll(gram[rows:], half, 1))
    return jnp.concatenate([top, moment], axis=0)


def unpacked(value, half):
    rows = half // 2
    lanes = lax.broadcasted_iota(jnp.int32, (half, 2 * half), 1)
    diagonal = lanes - half == lax.broadcasted_iota(jnp.int32, (half, 2 * half), 0)
    gram = jnp.concatenate([value[:rows], pltpu.roll(value[:rows], half, 1)], axis=0)
    return jnp.where(lanes < half, gram, diagonal.astype(jnp.float32))


def tree_kernel(spread, start, moment, work, local, sums, arrived, sent, landed):
    count, half, samples = start.shape
    depth = count.bit_length() - 1
    me = lax.axis_index(AXIS)
    bits = [lax.rem(lax.div(me, 1 << step), 2) for step in range(spread)]
    partners = [me + (1 - 2 * bit) * (1 << step) for step, bit in enumerate(bits)]
    barrier = pltpu.get_barrier_semaphore()
    for partner in partners:
        pl.semaphore_signal(barrier, inc=1, device_id=(partner,), device_id_type=MESH)

    def exchange(step):
        return pltpu.make_async_remote_copy(
            src_ref=sums.at[step],
            dst_ref=arrived.at[step],
            send_sem=sent.at[step],
            recv_sem=landed.at[step],
            device_id=(partners[step],),
            device_id_type=MESH,
        )

    grams = {(0, leaf): start[leaf] for leaf in range(count)}
    moments = {(0, leaf): moment[leaf] for leaf in range(count)}
    for height in range(1, depth + 1):
        for node in range(count >> height):
            for table in (grams, moments):
                table[height, node] = (
                    table[height - 1, 2 * node] + table[height - 1, 2 * node + 1]
                )
    sums[0] = packed(grams[depth, 0], moments[depth, 0])
    pl.semaphore_wait(barrier, spread)
    copies = [exchange(step) for step in range(spread)]
    copies[0].start()

    lanes = lax.broadcasted_iota(jnp.int32, (half, samples), 1)
    diagonal = lanes - half == lax.broadcasted_iota(jnp.int32, (half, samples), 0)
    for leaf in range(count):
        work[leaf] = start[leaf]
    place = count
    for height in range(1, depth + 1):
        local[height - 1] = moments[height, 0]
        for side in range(1 if height == depth else 2):
            work[place] = jnp.where(
                lanes < half, grams[height, side], diagonal.astype(jnp.float32)
            )
            place += 1
    octets = half // 8
    for step in range(spread):
        factor(
            work, 0, place, octets * step // spread, octets * (step + 1) // spread, 4
        )
        copies[step].wait()
        sums[step + 1] = sums[step] + arrived[step]
        if step + 1 < spread:
            copies[step + 1].start()


def tree_call(start, moment, spread):
    count, half, samples = start.shape
    depth = count.bit_length() - 1
    nodes = count + 2 * depth - 1
    rows = half // 2 + half
    vmem = pl.BlockSpec(memory_space=pltpu.VMEM)
    return pl.pallas_call(
        functools.partial(tree_kernel, spread),
        in_specs=[vmem] * 2,
        out_specs=[vmem] * 4,
        out_shape=[
            jax.ShapeDtypeStruct((nodes, half, samples), jnp.float32),
            jax.ShapeDtypeStruct((depth, half, samples), jnp.float32),
            jax.ShapeDtypeStruct((spread + 1, rows, samples), jnp.float32),
            jax.ShapeDtypeStruct((spread, rows, samples), jnp.float32),
        ],
        scratch_shapes=[
            pltpu.SemaphoreType.DMA((spread,)),
            pltpu.SemaphoreType.DMA((spread,)),
        ],
        compiler_params=pltpu.CompilerParams(
            collective_id=1, has_side_effects=True, vmem_limit_bytes=12 * 2**20
        ),
        name="tree",
    )(start, moment)


def out_kernel(work, moment, local, sums, arrived, compact, leaf_out, level_out, tops):
    count, half, samples = moment.shape
    depth = count.bit_length() - 1
    spread = arrived.shape[0]
    me = lax.axis_index(AXIS)
    lanes = lax.broadcasted_iota(jnp.int32, (half, samples), 1)
    triangle = lanes >= lax.broadcasted_iota(jnp.int32, (half, samples), 0)
    corner = triangle & (lanes < half)
    blank = jnp.zeros((half, samples), jnp.float32)

    def solved(matrix, right):
        middle = fine_dot(matrix, jnp.concatenate([blank, right], axis=0))
        return fine_dot(matrix, middle, ((0,), (0,)))[half:]

    def sketch(one, two, answer):
        stacked = jnp.concatenate(
            [jnp.where(corner, one, 0.0), jnp.where(corner, two, 0.0)], axis=0
        )
        return fine_dot(stacked, jnp.concatenate([answer, blank], axis=0))

    for step in range(spread):
        tops[2 * step] = unpacked(arrived[step], half)
        tops[2 * step + 1] = unpacked(sums[step + 1], half)
    factor(tops, 0, 2 * spread, 0, half // 8, 8)

    for leaf in range(count):
        answer = solved(work[leaf], moment[leaf])
        high = answer.astype(jnp.bfloat16)
        low = (answer - high.astype(jnp.float32)).astype(jnp.bfloat16)
        pair = jnp.concatenate([high, low], axis=1)
        both = jnp.dot(
            compact[leaf],
            jnp.concatenate([pair, pair], axis=0),
            preferred_element_type=jnp.float32,
        )
        leaf_out[leaf] = (both[:, :samples] + both[:, samples:]).astype(leaf_out.dtype)
    for height in range(1, depth + 1):
        first = 0 if height == 1 else count + 2 * (height - 2)
        answer = solved(work[count + 2 * (height - 1)], local[height - 1])
        level_out[0, height - 1] = sketch(work[first], work[first + 1], answer).astype(
            level_out.dtype
        )
    for step in range(spread):
        mine = work[count + 2 * (depth - 1)] if step == 0 else tops[2 * step - 1]
        other = tops[2 * step]
        odd = lax.rem(lax.div(me, 1 << step), 2) == 1
        answer = solved(tops[2 * step + 1], sums[step + 1, half // 2 :, :])
        level_out[0, depth + step] = sketch(
            jnp.where(odd, other, mine), jnp.where(odd, mine, other), answer
        ).astype(level_out.dtype)


def out_call(work, moment, local, sums, arrived, compact):
    count, rows, samples = compact.shape
    half = moment.shape[1]
    spread = arrived.shape[0]
    depth = count.bit_length() - 1
    vmem = pl.BlockSpec(memory_space=pltpu.VMEM)
    return pl.pallas_call(
        out_kernel,
        in_specs=[vmem] * 6,
        out_specs=[vmem] * 2,
        out_shape=[
            jax.ShapeDtypeStruct((count, rows, samples), jnp.bfloat16),
            jax.ShapeDtypeStruct((1, depth + spread, samples, samples), jnp.bfloat16),
        ],
        scratch_shapes=[pltpu.VMEM((2 * spread, half, samples), jnp.float32)],
        compiler_params=pltpu.CompilerParams(vmem_limit_bytes=12 * 2**20),
        name="out",
    )(work, moment, local, sums, arrived, compact)


def per_device(random_block, sample_block, near_blocks, near_index, near_count):
    spread = lax.axis_size(AXIS).bit_length() - 1
    index = near_index.T
    part, halo, held = halo_call(index, near_count, random_block, near_blocks, sample_block)
    start, moment, compact = gram_call(
        index, near_count, part, random_block, halo, held
    )
    work, local, sums, arrived = tree_call(start, moment, spread)
    return tuple(out_call(work, moment, local, sums, arrived, compact))


def solution(mesh):
    return jax.shard_map(
        per_device,
        mesh=mesh,
        in_specs=(
            P(AXIS, None, None),
            P(AXIS, None, None),
            P(AXIS, None, None, None),
            P(AXIS, None),
            P(AXIS),
        ),
        out_specs=(P(AXIS, None, None), P(AXIS, None, None, None)),
        check_vma=False,
    )
```

```python
import functools

import jax
import jax.numpy as jnp
from jax import lax
from jax.experimental import pallas as pl
from jax.experimental.pallas import tpu as pltpu
from jax.sharding import PartitionSpec as P

AXIS = "boxes"
MESH = pl.DeviceIdType.MESH


def fine_dot(a, b, dims=((1,), (0,))):
    return lax.dot_general(
        a, b, (dims, ((), ())), precision=lax.Precision.HIGH, preferred_element_type=jnp.float32
    )


def halo_kernel(
    lists,
    lengths,
    source,
    blocks,
    sample,
    part,
    halo,
    held,
    wide,
    base,
    index,
    counts,
    loads,
    arrivals,
    sent,
    landed,
):
    count, slots, rows = held.shape[:3]
    samples = part.shape[2]
    size = lax.axis_size(AXIS)
    me = lax.axis_index(AXIS)
    core = lax.rem(me, 2)
    partner = me + 1 - 2 * core
    across = me - 1 + 2 * core
    inside = (across >= 0) & (across < size)
    near_copy = pltpu.make_async_remote_copy(
        src_ref=source,
        dst_ref=wide.at[pl.ds(count, count)],
        send_sem=sent.at[0],
        recv_sem=landed.at[0],
        device_id=(partner,),
        device_id_type=MESH,
    )
    far_copy = pltpu.make_async_remote_copy(
        src_ref=source,
        dst_ref=halo,
        send_sem=sent.at[1],
        recv_sem=landed.at[1],
        device_id=(across,),
        device_id_type=MESH,
    )
    own_copy = pltpu.make_async_copy(source, wide.at[pl.ds(0, count)], loads.at[0])
    sample_copy = pltpu.make_async_copy(sample, base, loads.at[1])
    list_copy = pltpu.make_async_copy(lists, index, loads.at[2])
    length_copy = pltpu.make_async_copy(lengths, counts, loads.at[3])
    own_copies = (own_copy, sample_copy, list_copy, length_copy)

    def fetch(box):
        return pltpu.make_async_copy(blocks.at[box], held.at[box], arrivals.at[box])

    barrier = pltpu.get_barrier_semaphore()
    pl.semaphore_signal(barrier, inc=1, device_id=(partner,), device_id_type=MESH)

    @pl.when(inside)
    def _():
        pl.semaphore_signal(barrier, inc=1, device_id=(across,), device_id_type=MESH)
        pl.semaphore_wait(barrier, 2)
        far_copy.start()

    @pl.when(jnp.logical_not(inside))
    def _():
        pl.semaphore_wait(barrier, 1)

    near_copy.start()
    for copy in own_copies:
        copy.start()
    for box in range(count):
        fetch(box).start()
    for copy in own_copies:
        copy.wait()
    near_copy.wait()

    def near(box, carry):
        fetch(box).wait()
        picked = []
        for slot in range(slots):
            place = index[slot, box] - me * count
            other = place - (1 - 2 * core) * count
            own = (place >= 0) & (place < count)
            beside = (other >= 0) & (other < count)
            pick = jnp.where(own, place, jnp.where(beside, other + count, 0))
            keep = ((own | beside) & (slot < counts[box])).astype(jnp.float32)
            picked.append(wide[pick] * keep.astype(jnp.bfloat16))
        part[box] = base[box].astype(jnp.float32) - jnp.dot(
            jnp.concatenate([held[box, slot] for slot in range(slots)], axis=1),
            jnp.concatenate(picked, axis=0),
            preferred_element_type=jnp.float32,
        )
        return carry

    lax.fori_loop(0, count, near, 0)

    @pl.when(inside)
    def _():
        far_copy.wait()


def halo_call(index, counts, source, blocks, sample):
    count, rows, samples = sample.shape
    anywhere = pl.BlockSpec(memory_space=pl.ANY)
    fixed = pl.BlockSpec(memory_space=pltpu.HBM)
    vmem = pl.BlockSpec(memory_space=pltpu.VMEM)
    return pl.pallas_call(
        halo_kernel,
        in_specs=[fixed] * 5,
        out_specs=[vmem, anywhere, vmem],
        out_shape=[
            jax.ShapeDtypeStruct(sample.shape, jnp.float32),
            jax.ShapeDtypeStruct(sample.shape, jnp.bfloat16),
            jax.ShapeDtypeStruct(blocks.shape, jnp.bfloat16),
        ],
        scratch_shapes=[
            pltpu.VMEM((2 * count, rows, samples), jnp.bfloat16),
            pltpu.VMEM((count, rows, samples), jnp.bfloat16),
            pltpu.SMEM(index.shape, jnp.int32),
            pltpu.SMEM(counts.shape, jnp.int32),
            pltpu.SemaphoreType.DMA((4,)),
            pltpu.SemaphoreType.DMA((count,)),
            pltpu.SemaphoreType.DMA((2,)),
            pltpu.SemaphoreType.DMA((2,)),
        ],
        compiler_params=pltpu.CompilerParams(
            collective_id=0, has_side_effects=True, vmem_limit_bytes=30 * 2**20
        ),
        name="halo",
    )(index, counts, source, blocks, sample)


def gram_kernel(
    index, counts, part, source, halo, blocks, start, moment, compact, far, picks
):
    count, rows, samples = far.shape
    slots = blocks.shape[1]
    half = samples // 2
    me = lax.axis_index(AXIS)
    core = lax.rem(me, 2)
    base = (me - 1 + 2 * core) * count

    found = jnp.int32(0)
    for box in range(count):
        far[box] = part[box]
        for slot in range(1, slots):
            place = index[slot, box] - base
            needed = (place >= 0) & (place < count) & (slot < counts[box])
            picks[found] = (box * slots + slot) * count + place
            found = found + needed.astype(jnp.int32)
    group = 4

    def multiply(turn, carry):
        terms = []
        for member in range(group):
            entry = turn * group + member
            code = picks[jnp.minimum(entry, found - 1)]
            block = lax.div(code, count)
            box = lax.div(block, slots)
            keep = (entry < found).astype(jnp.float32).astype(jnp.bfloat16)
            terms.append(
                (
                    box,
                    jnp.dot(
                        blocks[box, lax.rem(block, slots)],
                        halo[lax.rem(code, count)] * keep,
                        preferred_element_type=jnp.float32,
                    ),
                )
            )
        for box, term in terms:
            far[box] -= term
        return carry

    lax.fori_loop(0, lax.div(found + group - 1, group), multiply, 0)

    lanes_rows = lax.broadcasted_iota(jnp.int32, (rows, samples), 1)
    lanes = lax.broadcasted_iota(jnp.int32, (half, samples), 1)
    diagonal = lanes - half == lax.broadcasted_iota(jnp.int32, (half, samples), 0)
    together = 4 if count % 4 == 0 else 1

    def reduce(turn, carry):
        for member in range(together):
            box = turn * together + member
            value = far[box]
            doubled = value + pltpu.roll(value, half, 1)
            high = doubled.astype(jnp.bfloat16).astype(jnp.float32)
            both = jnp.where(lanes_rows < half, high, doubled - high).astype(jnp.bfloat16)
            compact[box] = both
            product = jnp.dot(
                both.T,
                jnp.concatenate([source[box], both], axis=1),
                preferred_element_type=jnp.float32,
            )
            moment[box] = product[:half, :samples] + product[half:, :samples]
            mixed = product[:half, samples:] + product[half:, samples:]
            start[box] = jnp.where(
                lanes < half, mixed + pltpu.roll(mixed, half, 1), diagonal.astype(jnp.float32)
            )
        return carry

    lax.fori_loop(0, count // together, reduce, 0)


def gram_call(index, counts, part, source, halo, blocks):
    count, rows, samples = part.shape
    slots = blocks.shape[1]
    half = samples // 2
    most = count * (slots - 1)
    smem = pl.BlockSpec(memory_space=pltpu.SMEM)
    vmem = pl.BlockSpec(memory_space=pltpu.VMEM)
    return pl.pallas_call(
        gram_kernel,
        in_specs=[smem, smem, vmem, vmem, vmem, vmem],
        out_specs=[vmem] * 3,
        out_shape=[
            jax.ShapeDtypeStruct((count, half, samples), jnp.float32),
            jax.ShapeDtypeStruct((count, half, samples), jnp.float32),
            jax.ShapeDtypeStruct((count, rows, samples), jnp.bfloat16),
        ],
        scratch_shapes=[
            pltpu.VMEM((count, rows, samples), jnp.float32),
            pltpu.SMEM((most + 1,), jnp.int32),
        ],
        compiler_params=pltpu.CompilerParams(vmem_limit_bytes=12 * 2**20),
        name="gram",
    )(index, counts, part, source, halo, blocks)


def factor(work, first, nodes, low, high, width):
    half, samples = work.shape[1:]
    octets = half // 8
    row8 = lax.broadcasted_iota(jnp.int32, (nodes, 8, samples), 1)

    def spread_row(value, row):
        return jnp.broadcast_to(value[:, row : row + 1, :], value.shape)

    def spread_column(value, lane):
        flat = value.reshape(nodes * 8, samples)
        return jnp.broadcast_to(flat[:, lane : lane + 1], flat.shape).reshape(value.shape)

    def octet(place):
        return work[first : first + nodes, 8 * place : 8 * place + 8, :]

    def put(place, value):
        work[first : first + nodes, 8 * place : 8 * place + 8, :] = value

    for place in range(low, high):
        base = 8 * place
        head = octet(place)
        upper, pivots = head, None
        for begin in range(0, 8, width):
            rows = range(begin, begin + width)
            columns = {row: spread_column(head, base + row) for row in rows}
            for row in rows:
                pivot = spread_row(columns[row], row)
                pivots = pivot if pivots is None else jnp.where(row8 == row, pivot, pivots)
                scaled = jnp.where(row8 == row, 0.0, columns[row] * (1.0 / pivot))
                line = spread_row(head, row)
                if row:
                    upper = jnp.where(row8 == row, line, upper)
                head = head - scaled * line
                for later in range(row + 1, begin + width):
                    columns[later] = columns[later] - scaled * spread_row(columns[later], row)
        put(place, upper * lax.rsqrt(pivots))
        if place + 1 == octets:
            break
        head = head * (1.0 / pivots)
        lines = [spread_row(head, row) for row in range(8)]
        for other in range(place + 1, octets):
            value = octet(other)
            columns = [spread_column(value, base + row) for row in range(8)]
            for row in range(8):
                value = value - columns[row] * lines[row]
            put(other, value)


def packed(gram, moment):
    rows = gram.shape[0] // 2
    half = gram.shape[1] // 2
    lanes = lax.broadcasted_iota(jnp.int32, (rows, 2 * half), 1)
    top = jnp.where(lanes < half, gram[:rows], pltpu.roll(gram[rows:], half, 1))
    return jnp.concatenate([top, moment], axis=0)


def unpacked(value, half):
    rows = half // 2
    lanes = lax.broadcasted_iota(jnp.int32, (half, 2 * half), 1)
    diagonal = lanes - half == lax.broadcasted_iota(jnp.int32, (half, 2 * half), 0)
    gram = jnp.concatenate([value[:rows], pltpu.roll(value[:rows], half, 1)], axis=0)
    return jnp.where(lanes < half, gram, diagonal.astype(jnp.float32))


def tree_kernel(spread, start, moment, work, local, sums, arrived, sent, landed):
    count, half, samples = start.shape
    depth = count.bit_length() - 1
    me = lax.axis_index(AXIS)
    bits = [lax.rem(lax.div(me, 1 << step), 2) for step in range(spread)]
    partners = [me + (1 - 2 * bit) * (1 << step) for step, bit in enumerate(bits)]
    barrier = pltpu.get_barrier_semaphore()
    for partner in partners:
        pl.semaphore_signal(barrier, inc=1, device_id=(partner,), device_id_type=MESH)

    def exchange(step):
        return pltpu.make_async_remote_copy(
            src_ref=sums.at[step],
            dst_ref=arrived.at[step],
            send_sem=sent.at[step],
            recv_sem=landed.at[step],
            device_id=(partners[step],),
            device_id_type=MESH,
        )

    grams = {(0, leaf): start[leaf] for leaf in range(count)}
    moments = {(0, leaf): moment[leaf] for leaf in range(count)}
    for height in range(1, depth + 1):
        for node in range(count >> height):
            for table in (grams, moments):
                table[height, node] = (
                    table[height - 1, 2 * node] + table[height - 1, 2 * node + 1]
                )
    sums[0] = packed(grams[depth, 0], moments[depth, 0])
    pl.semaphore_wait(barrier, spread)
    copies = [exchange(step) for step in range(spread)]
    copies[0].start()

    lanes = lax.broadcasted_iota(jnp.int32, (half, samples), 1)
    diagonal = lanes - half == lax.broadcasted_iota(jnp.int32, (half, samples), 0)
    for leaf in range(count):
        work[leaf] = start[leaf]
    place = count
    for height in range(1, depth + 1):
        local[height - 1] = moments[height, 0]
        for side in range(1 if height == depth else 2):
            work[place] = jnp.where(
                lanes < half, grams[height, side], diagonal.astype(jnp.float32)
            )
            place += 1
    octets = half // 8
    for step in range(spread):
        factor(
            work, 0, place, octets * step // spread, octets * (step + 1) // spread, 4
        )
        copies[step].wait()
        sums[step + 1] = sums[step] + arrived[step]
        if step + 1 < spread:
            copies[step + 1].start()


def tree_call(start, moment, spread):
    count, half, samples = start.shape
    depth = count.bit_length() - 1
    nodes = count + 2 * depth - 1
    rows = half // 2 + half
    vmem = pl.BlockSpec(memory_space=pltpu.VMEM)
    return pl.pallas_call(
        functools.partial(tree_kernel, spread),
        in_specs=[vmem] * 2,
        out_specs=[vmem] * 4,
        out_shape=[
            jax.ShapeDtypeStruct((nodes, half, samples), jnp.float32),
            jax.ShapeDtypeStruct((depth, half, samples), jnp.float32),
            jax.ShapeDtypeStruct((spread + 1, rows, samples), jnp.float32),
            jax.ShapeDtypeStruct((spread, rows, samples), jnp.float32),
        ],
        scratch_shapes=[
            pltpu.SemaphoreType.DMA((spread,)),
            pltpu.SemaphoreType.DMA((spread,)),
        ],
        compiler_params=pltpu.CompilerParams(
            collective_id=1, has_side_effects=True, vmem_limit_bytes=12 * 2**20
        ),
        name="tree",
    )(start, moment)


def out_kernel(work, moment, local, sums, arrived, compact, leaf_out, level_out, tops):
    count, half, samples = moment.shape
    depth = count.bit_length() - 1
    spread = arrived.shape[0]
    me = lax.axis_index(AXIS)
    lanes = lax.broadcasted_iota(jnp.int32, (half, samples), 1)
    triangle = lanes >= lax.broadcasted_iota(jnp.int32, (half, samples), 0)
    corner = triangle & (lanes < half)
    blank = jnp.zeros((half, samples), jnp.float32)

    def solved(matrix, right):
        middle = fine_dot(matrix, jnp.concatenate([blank, right], axis=0))
        return fine_dot(matrix, middle, ((0,), (0,)))[half:]

    def sketch(one, two, answer):
        stacked = jnp.concatenate(
            [jnp.where(corner, one, 0.0), jnp.where(corner, two, 0.0)], axis=0
        )
        return fine_dot(stacked, jnp.concatenate([answer, blank], axis=0))

    for step in range(spread):
        tops[2 * step] = unpacked(arrived[step], half)
        tops[2 * step + 1] = unpacked(sums[step + 1], half)
    octets = half // 8
    for turn in range(octets):
        factor(tops, 0, 2 * spread, turn, turn + 1, 8)
        for leaf in range(count * turn // octets, count * (turn + 1) // octets):
            answer = solved(work[leaf], moment[leaf])
            high = answer.astype(jnp.bfloat16)
            low = (answer - high.astype(jnp.float32)).astype(jnp.bfloat16)
            pair = jnp.concatenate([high, low], axis=1)
            both = jnp.dot(
                compact[leaf],
                jnp.concatenate([pair, pair], axis=0),
                preferred_element_type=jnp.float32,
            )
            leaf_out[leaf] = (both[:, :samples] + both[:, samples:]).astype(leaf_out.dtype)
    for height in range(1, depth + 1):
        first = 0 if height == 1 else count + 2 * (height - 2)
        answer = solved(work[count + 2 * (height - 1)], local[height - 1])
        level_out[0, height - 1] = sketch(work[first], work[first + 1], answer).astype(
            level_out.dtype
        )
    for step in range(spread):
        mine = work[count + 2 * (depth - 1)] if step == 0 else tops[2 * step - 1]
        other = tops[2 * step]
        odd = lax.rem(lax.div(me, 1 << step), 2) == 1
        answer = solved(tops[2 * step + 1], sums[step + 1, half // 2 :, :])
        level_out[0, depth + step] = sketch(
            jnp.where(odd, other, mine), jnp.where(odd, mine, other), answer
        ).astype(level_out.dtype)


def out_call(work, moment, local, sums, arrived, compact):
    count, rows, samples = compact.shape
    half = moment.shape[1]
    spread = arrived.shape[0]
    depth = count.bit_length() - 1
    vmem = pl.BlockSpec(memory_space=pltpu.VMEM)
    return pl.pallas_call(
        out_kernel,
        in_specs=[vmem] * 6,
        out_specs=[vmem] * 2,
        out_shape=[
            jax.ShapeDtypeStruct((count, rows, samples), jnp.bfloat16),
            jax.ShapeDtypeStruct((1, depth + spread, samples, samples), jnp.bfloat16),
        ],
        scratch_shapes=[pltpu.VMEM((2 * spread, half, samples), jnp.float32)],
        compiler_params=pltpu.CompilerParams(vmem_limit_bytes=12 * 2**20),
        name="out",
    )(work, moment, local, sums, arrived, compact)


def per_device(random_block, sample_block, near_blocks, near_index, near_count):
    spread = lax.axis_size(AXIS).bit_length() - 1
    index = near_index.T
    fixed = [
        pltpu.with_memory_space_constraint(value, pltpu.HBM)
        for value in (index, near_count, random_block, near_blocks, sample_block)
    ]
    part, halo, held = halo_call(*fixed)
    start, moment, compact = gram_call(
        index, near_count, part, random_block, halo, held
    )
    work, local, sums, arrived = tree_call(start, moment, spread)
    return tuple(out_call(work, moment, local, sums, arrived, compact))


def solution(mesh):
    return jax.shard_map(
        per_device,
        mesh=mesh,
        in_specs=(
            P(AXIS, None, None),
            P(AXIS, None, None),
            P(AXIS, None, None, None),
            P(AXIS, None),
            P(AXIS),
        ),
        out_specs=(P(AXIS, None, None), P(AXIS, None, None, None)),
        check_vma=False,
    )
```

```python
import functools

import jax
import jax.numpy as jnp
from jax import lax
from jax.experimental import pallas as pl
from jax.experimental.pallas import tpu as pltpu
from jax.sharding import PartitionSpec as P

AXIS = "boxes"
MESH = pl.DeviceIdType.MESH


def fine_dot(a, b, dims=((1,), (0,))):
    return lax.dot_general(
        a, b, (dims, ((), ())), precision=lax.Precision.HIGH, preferred_element_type=jnp.float32
    )


def halo_kernel(
    lists,
    lengths,
    source,
    blocks,
    sample,
    part,
    halo,
    held,
    wide,
    base,
    index,
    counts,
    loads,
    arrivals,
    sent,
    landed,
):
    count, slots, rows = held.shape[:3]
    samples = part.shape[2]
    size = lax.axis_size(AXIS)
    me = lax.axis_index(AXIS)
    core = lax.rem(me, 2)
    partner = me + 1 - 2 * core
    across = me - 1 + 2 * core
    inside = (across >= 0) & (across < size)
    near_copy = pltpu.make_async_remote_copy(
        src_ref=source,
        dst_ref=wide.at[pl.ds(count, count)],
        send_sem=sent.at[0],
        recv_sem=landed.at[0],
        device_id=(partner,),
        device_id_type=MESH,
    )
    far_copy = pltpu.make_async_remote_copy(
        src_ref=source,
        dst_ref=halo,
        send_sem=sent.at[1],
        recv_sem=landed.at[1],
        device_id=(across,),
        device_id_type=MESH,
    )
    own_copy = pltpu.make_async_copy(source, wide.at[pl.ds(0, count)], loads.at[0])
    sample_copy = pltpu.make_async_copy(sample, base, loads.at[1])
    list_copy = pltpu.make_async_copy(lists, index, loads.at[2])
    length_copy = pltpu.make_async_copy(lengths, counts, loads.at[3])
    own_copies = (own_copy, sample_copy, list_copy, length_copy)

    def fetch(box):
        return pltpu.make_async_copy(blocks.at[box], held.at[box], arrivals.at[box])

    barrier = pltpu.get_barrier_semaphore()
    pl.semaphore_signal(barrier, inc=1, device_id=(partner,), device_id_type=MESH)

    @pl.when(inside)
    def _():
        pl.semaphore_signal(barrier, inc=1, device_id=(across,), device_id_type=MESH)
        pl.semaphore_wait(barrier, 2)
        far_copy.start()

    @pl.when(jnp.logical_not(inside))
    def _():
        pl.semaphore_wait(barrier, 1)

    near_copy.start()
    for copy in own_copies:
        copy.start()
    for box in range(count):
        fetch(box).start()
    for copy in own_copies:
        copy.wait()
    near_copy.wait()

    def near(box, carry):
        fetch(box).wait()
        picked = []
        for slot in range(slots):
            place = index[slot, box] - me * count
            other = place - (1 - 2 * core) * count
            own = (place >= 0) & (place < count)
            beside = (other >= 0) & (other < count)
            pick = jnp.where(own, place, jnp.where(beside, other + count, 0))
            keep = ((own | beside) & (slot < counts[box])).astype(jnp.float32)
            picked.append(wide[pick] * keep.astype(jnp.bfloat16))
        part[box] = base[box].astype(jnp.float32) - jnp.dot(
            jnp.concatenate([held[box, slot] for slot in range(slots)], axis=1),
            jnp.concatenate(picked, axis=0),
            preferred_element_type=jnp.float32,
        )
        return carry

    lax.fori_loop(0, count, near, 0)

    @pl.when(inside)
    def _():
        far_copy.wait()


def halo_call(index, counts, source, blocks, sample):
    count, rows, samples = sample.shape
    anywhere = pl.BlockSpec(memory_space=pl.ANY)
    fixed = pl.BlockSpec(memory_space=pltpu.HBM)
    vmem = pl.BlockSpec(memory_space=pltpu.VMEM)
    return pl.pallas_call(
        halo_kernel,
        in_specs=[fixed] * 5,
        out_specs=[vmem, anywhere, vmem],
        out_shape=[
            jax.ShapeDtypeStruct(sample.shape, jnp.float32),
            jax.ShapeDtypeStruct(sample.shape, jnp.bfloat16),
            jax.ShapeDtypeStruct(blocks.shape, jnp.bfloat16),
        ],
        scratch_shapes=[
            pltpu.VMEM((2 * count, rows, samples), jnp.bfloat16),
            pltpu.VMEM((count, rows, samples), jnp.bfloat16),
            pltpu.SMEM(index.shape, jnp.int32),
            pltpu.SMEM(counts.shape, jnp.int32),
            pltpu.SemaphoreType.DMA((4,)),
            pltpu.SemaphoreType.DMA((count,)),
            pltpu.SemaphoreType.DMA((2,)),
            pltpu.SemaphoreType.DMA((2,)),
        ],
        compiler_params=pltpu.CompilerParams(
            collective_id=0, has_side_effects=True, vmem_limit_bytes=30 * 2**20
        ),
        name="halo",
    )(index, counts, source, blocks, sample)


def gram_kernel(
    index, counts, part, source, halo, blocks, start, moment, compact, far, picks
):
    count, rows, samples = far.shape
    slots = blocks.shape[1]
    half = samples // 2
    me = lax.axis_index(AXIS)
    core = lax.rem(me, 2)
    base = (me - 1 + 2 * core) * count

    found = jnp.int32(0)
    for box in range(count):
        far[box] = part[box]
        for slot in range(1, slots):
            place = index[slot, box] - base
            needed = (place >= 0) & (place < count) & (slot < counts[box])
            picks[found] = (box * slots + slot) * count + place
            found = found + needed.astype(jnp.int32)
    group = 4

    def multiply(turn, carry):
        terms = []
        for member in range(group):
            entry = turn * group + member
            code = picks[jnp.minimum(entry, found - 1)]
            block = lax.div(code, count)
            box = lax.div(block, slots)
            keep = (entry < found).astype(jnp.float32).astype(jnp.bfloat16)
            terms.append(
                (
                    box,
                    jnp.dot(
                        blocks[box, lax.rem(block, slots)],
                        halo[lax.rem(code, count)] * keep,
                        preferred_element_type=jnp.float32,
                    ),
                )
            )
        for box, term in terms:
            far[box] -= term
        return carry

    lax.fori_loop(0, lax.div(found + group - 1, group), multiply, 0)

    lanes_rows = lax.broadcasted_iota(jnp.int32, (rows, samples), 1)
    lanes = lax.broadcasted_iota(jnp.int32, (half, samples), 1)
    diagonal = lanes - half == lax.broadcasted_iota(jnp.int32, (half, samples), 0)
    together = 4 if count % 4 == 0 else 1

    def reduce(turn, carry):
        for member in range(together):
            box = turn * together + member
            value = far[box]
            doubled = value + pltpu.roll(value, half, 1)
            high = doubled.astype(jnp.bfloat16).astype(jnp.float32)
            both = jnp.where(lanes_rows < half, high, doubled - high).astype(jnp.bfloat16)
            compact[box] = both
            product = jnp.dot(
                both.T,
                jnp.concatenate([source[box], both], axis=1),
                preferred_element_type=jnp.float32,
            )
            moment[box] = product[:half, :samples] + product[half:, :samples]
            mixed = product[:half, samples:] + product[half:, samples:]
            start[box] = jnp.where(
                lanes < half, mixed + pltpu.roll(mixed, half, 1), diagonal.astype(jnp.float32)
            )
        return carry

    lax.fori_loop(0, count // together, reduce, 0)


def gram_call(index, counts, part, source, halo, blocks):
    count, rows, samples = part.shape
    slots = blocks.shape[1]
    half = samples // 2
    most = count * (slots - 1)
    smem = pl.BlockSpec(memory_space=pltpu.SMEM)
    vmem = pl.BlockSpec(memory_space=pltpu.VMEM)
    return pl.pallas_call(
        gram_kernel,
        in_specs=[smem, smem, vmem, vmem, vmem, vmem],
        out_specs=[vmem] * 3,
        out_shape=[
            jax.ShapeDtypeStruct((count, half, samples), jnp.float32),
            jax.ShapeDtypeStruct((count, half, samples), jnp.float32),
            jax.ShapeDtypeStruct((count, rows, samples), jnp.bfloat16),
        ],
        scratch_shapes=[
            pltpu.VMEM((count, rows, samples), jnp.float32),
            pltpu.SMEM((most + 1,), jnp.int32),
        ],
        compiler_params=pltpu.CompilerParams(vmem_limit_bytes=12 * 2**20),
        name="gram",
    )(index, counts, part, source, halo, blocks)


def factor(work, nodes, low, high, width):
    half, samples = work.shape[1:]
    octets = half // 8
    row8 = lax.broadcasted_iota(jnp.int32, (nodes, 8, samples), 1)

    def spread_row(value, row):
        return jnp.broadcast_to(value[:, row : row + 1, :], value.shape)

    def spread_column(value, lane):
        flat = value.reshape(nodes * 8, samples)
        return jnp.broadcast_to(flat[:, lane : lane + 1], flat.shape).reshape(value.shape)

    for place in range(low, high):
        base = 8 * place
        head = work[:nodes, base : base + 8, :]
        pivots = None
        for begin in range(0, 8, width):
            rows = range(begin, begin + width)
            columns = {row: spread_column(head, base + row) for row in rows}
            for row in rows:
                pivot = spread_row(columns[row], row)
                pivots = pivot if pivots is None else jnp.where(row8 >= row, pivot, pivots)
                if row == 7:
                    break
                scaled = jnp.where(row8 > row, columns[row] * (1.0 / pivot), 0.0)
                head = head - scaled * spread_row(head, row)
                for later in range(row + 1, begin + width):
                    columns[later] = columns[later] - scaled * spread_row(columns[later], row)
        root = head * lax.rsqrt(pivots)
        work[:nodes, base : base + 8, :] = root
        if place + 1 == octets:
            break
        high_part = root.astype(jnp.bfloat16).astype(jnp.float32)
        rest = root - high_part
        middle = rest.astype(jnp.bfloat16).astype(jnp.float32)
        low_part = rest - middle
        for node in range(nodes):
            h, m, t = high_part[node], middle[node], low_part[node]
            left = jnp.concatenate([h, h, m, m, h, t], axis=0).astype(jnp.bfloat16)
            right = jnp.concatenate([h, m, h, m, t, h], axis=0).astype(jnp.bfloat16)
            update = lax.dot_general(
                left[:, :half],
                right,
                (((0,), (0,)), ((), ())),
                preferred_element_type=jnp.float32,
            )
            work[node, base + 8 :, :] = work[node, base + 8 :, :] - update[base + 8 :, :]


def solved(matrix, right):
    half = right.shape[0]
    blank = jnp.zeros_like(right)
    middle = fine_dot(matrix, jnp.concatenate([blank, right], axis=0))
    return fine_dot(matrix, middle, ((0,), (0,)))[half:]


def packed(gram, moment):
    rows = gram.shape[0] // 2
    half = gram.shape[1] // 2
    lanes = lax.broadcasted_iota(jnp.int32, (rows, 2 * half), 1)
    top = jnp.where(lanes < half, gram[:rows], pltpu.roll(gram[rows:], half, 1))
    return jnp.concatenate([top, moment], axis=0)


def unpacked(value, half):
    rows = half // 2
    lanes = lax.broadcasted_iota(jnp.int32, (half, 2 * half), 1)
    diagonal = lanes - half == lax.broadcasted_iota(jnp.int32, (half, 2 * half), 0)
    gram = jnp.concatenate([value[:rows], pltpu.roll(value[:rows], half, 1)], axis=0)
    return jnp.where(lanes < half, gram, diagonal.astype(jnp.float32))


def tree_kernel(spread, start, moment, work, answers, sums, arrived, sent, landed):
    count, half, samples = start.shape
    depth = count.bit_length() - 1
    me = lax.axis_index(AXIS)
    bits = [lax.rem(lax.div(me, 1 << step), 2) for step in range(spread)]
    partners = [me + (1 - 2 * bit) * (1 << step) for step, bit in enumerate(bits)]
    barrier = pltpu.get_barrier_semaphore()
    for partner in partners:
        pl.semaphore_signal(barrier, inc=1, device_id=(partner,), device_id_type=MESH)

    def exchange(step):
        return pltpu.make_async_remote_copy(
            src_ref=sums.at[step],
            dst_ref=arrived.at[step],
            send_sem=sent.at[step],
            recv_sem=landed.at[step],
            device_id=(partners[step],),
            device_id_type=MESH,
        )

    grams = {(0, leaf): start[leaf] for leaf in range(count)}
    moments = {(0, leaf): moment[leaf] for leaf in range(count)}
    for height in range(1, depth + 1):
        for node in range(count >> height):
            for table in (grams, moments):
                table[height, node] = (
                    table[height - 1, 2 * node] + table[height - 1, 2 * node + 1]
                )
    sums[0] = packed(grams[depth, 0], moments[depth, 0])
    pl.semaphore_wait(barrier, spread)
    copies = [exchange(step) for step in range(spread)]
    copies[0].start()

    lanes = lax.broadcasted_iota(jnp.int32, (half, samples), 1)
    diagonal = lanes - half == lax.broadcasted_iota(jnp.int32, (half, samples), 0)
    for leaf in range(count):
        work[leaf] = start[leaf]
    place = count
    targets = [(leaf, moments[0, leaf]) for leaf in range(count)]
    for height in range(1, depth + 1):
        targets.append((place, moments[height, 0]))
        for side in range(1 if height == depth else 2):
            work[place] = jnp.where(
                lanes < half, grams[height, side], diagonal.astype(jnp.float32)
            )
            place += 1
    octets = half // 8
    turns = max(spread - 1, 1)
    for step in range(spread):
        if step < turns:
            factor(work, place, octets * step // turns, octets * (step + 1) // turns, 4)
        if step == spread - 1:
            for row, (node, right) in enumerate(targets):
                answers[row] = solved(work[node], right)
        copies[step].wait()
        sums[step + 1] = sums[step] + arrived[step]
        if step + 1 < spread:
            copies[step + 1].start()


def tree_call(start, moment, spread):
    count, half, samples = start.shape
    depth = count.bit_length() - 1
    nodes = count + 2 * depth - 1
    rows = half // 2 + half
    vmem = pl.BlockSpec(memory_space=pltpu.VMEM)
    return pl.pallas_call(
        functools.partial(tree_kernel, spread),
        in_specs=[vmem] * 2,
        out_specs=[vmem] * 4,
        out_shape=[
            jax.ShapeDtypeStruct((nodes, half, samples), jnp.float32),
            jax.ShapeDtypeStruct((count + depth, half, samples), jnp.float32),
            jax.ShapeDtypeStruct((spread + 1, rows, samples), jnp.float32),
            jax.ShapeDtypeStruct((spread, rows, samples), jnp.float32),
        ],
        scratch_shapes=[
            pltpu.SemaphoreType.DMA((spread,)),
            pltpu.SemaphoreType.DMA((spread,)),
        ],
        compiler_params=pltpu.CompilerParams(
            collective_id=1, has_side_effects=True, vmem_limit_bytes=12 * 2**20
        ),
        name="tree",
    )(start, moment)


def out_kernel(
    work, answers, sums, arrived, compact, leaf_out, level_out, tops, leaves, sems
):
    count, rows, samples = compact.shape
    half = answers.shape[1]
    depth = count.bit_length() - 1
    spread = arrived.shape[0]
    me = lax.axis_index(AXIS)
    lanes = lax.broadcasted_iota(jnp.int32, (half, samples), 1)
    triangle = lanes >= lax.broadcasted_iota(jnp.int32, (half, samples), 0)
    corner = triangle & (lanes < half)
    blank = jnp.zeros((half, samples), jnp.float32)

    def sketch(one, two, answer):
        stacked = jnp.concatenate(
            [jnp.where(corner, one, 0.0), jnp.where(corner, two, 0.0)], axis=0
        )
        return fine_dot(stacked, jnp.concatenate([answer, blank], axis=0))

    for step in range(spread):
        tops[2 * step] = unpacked(arrived[step], half)
        tops[2 * step + 1] = unpacked(sums[step + 1], half)
    octets = half // 8
    copies = []
    for turn in range(octets):
        factor(tops, 2 * spread, turn, turn + 1, 8)
        first, last = count * turn // octets, count * (turn + 1) // octets
        for leaf in range(first, last):
            answer = answers[leaf]
            high = answer.astype(jnp.bfloat16)
            low = (answer - high.astype(jnp.float32)).astype(jnp.bfloat16)
            pair = jnp.concatenate([high, low], axis=1)
            both = jnp.dot(
                compact[leaf],
                jnp.concatenate([pair, pair], axis=0),
                preferred_element_type=jnp.float32,
            )
            leaves[leaf] = (both[:, :samples] + both[:, samples:]).astype(leaves.dtype)
        if last > first:
            part = pl.ds(first, last - first)
            copy = pltpu.make_async_copy(leaves.at[part], leaf_out.at[part], sems.at[turn])
            copy.start()
            copies.append(copy)
    for height in range(1, depth + 1):
        first = 0 if height == 1 else count + 2 * (height - 2)
        level_out[0, height - 1] = sketch(
            work[first], work[first + 1], answers[count + height - 1]
        ).astype(level_out.dtype)
    for step in range(spread):
        mine = work[count + 2 * (depth - 1)] if step == 0 else tops[2 * step - 1]
        other = tops[2 * step]
        odd = lax.rem(lax.div(me, 1 << step), 2) == 1
        answer = solved(tops[2 * step + 1], sums[step + 1, half // 2 :, :])
        level_out[0, depth + step] = sketch(
            jnp.where(odd, other, mine), jnp.where(odd, mine, other), answer
        ).astype(level_out.dtype)
    for copy in copies:
        copy.wait()


def out_call(work, answers, sums, arrived, compact):
    count, rows, samples = compact.shape
    half = answers.shape[1]
    spread = arrived.shape[0]
    depth = count.bit_length() - 1
    vmem = pl.BlockSpec(memory_space=pltpu.VMEM)
    return pl.pallas_call(
        out_kernel,
        in_specs=[vmem] * 5,
        out_specs=[pl.BlockSpec(memory_space=pl.ANY), vmem],
        out_shape=[
            jax.ShapeDtypeStruct((count, rows, samples), jnp.bfloat16),
            jax.ShapeDtypeStruct((1, depth + spread, samples, samples), jnp.bfloat16),
        ],
        scratch_shapes=[
            pltpu.VMEM((2 * spread, half, samples), jnp.float32),
            pltpu.VMEM((count, rows, samples), jnp.bfloat16),
            pltpu.SemaphoreType.DMA((half // 8,)),
        ],
        compiler_params=pltpu.CompilerParams(vmem_limit_bytes=12 * 2**20),
        name="out",
    )(work, answers, sums, arrived, compact)


def per_device(random_block, sample_block, near_blocks, near_index, near_count):
    spread = lax.axis_size(AXIS).bit_length() - 1
    index = near_index.T
    fixed = [
        pltpu.with_memory_space_constraint(value, pltpu.HBM)
        for value in (index, near_count, random_block, near_blocks, sample_block)
    ]
    part, halo, held = halo_call(*fixed)
    start, moment, compact = gram_call(
        index, near_count, part, random_block, halo, held
    )
    work, answers, sums, arrived = tree_call(start, moment, spread)
    return tuple(out_call(work, answers, sums, arrived, compact))


def solution(mesh):
    return jax.shard_map(
        per_device,
        mesh=mesh,
        in_specs=(
            P(AXIS, None, None),
            P(AXIS, None, None),
            P(AXIS, None, None, None),
            P(AXIS, None),
            P(AXIS),
        ),
        out_specs=(P(AXIS, None, None), P(AXIS, None, None, None)),
        check_vma=False,
    )
```

```python
import functools

import jax
import jax.numpy as jnp
from jax import lax
from jax.experimental import pallas as pl
from jax.experimental.pallas import tpu as pltpu
from jax.sharding import PartitionSpec as P

AXIS = "boxes"
MESH = pl.DeviceIdType.MESH


def fine_dot(a, b, dims=((1,), (0,))):
    return lax.dot_general(
        a, b, (dims, ((), ())), precision=lax.Precision.HIGH, preferred_element_type=jnp.float32
    )


def halo_kernel(
    lists,
    lengths,
    source,
    blocks,
    sample,
    part,
    halo,
    held,
    wide,
    base,
    index,
    counts,
    loads,
    arrivals,
    sent,
    landed,
):
    count, slots, rows = held.shape[:3]
    samples = part.shape[2]
    size = lax.axis_size(AXIS)
    me = lax.axis_index(AXIS)
    core = lax.rem(me, 2)
    partner = me + 1 - 2 * core
    across = me - 1 + 2 * core
    inside = (across >= 0) & (across < size)
    near_copy = pltpu.make_async_remote_copy(
        src_ref=source,
        dst_ref=wide.at[pl.ds(count, count)],
        send_sem=sent.at[0],
        recv_sem=landed.at[0],
        device_id=(partner,),
        device_id_type=MESH,
    )
    far_copy = pltpu.make_async_remote_copy(
        src_ref=source,
        dst_ref=halo,
        send_sem=sent.at[1],
        recv_sem=landed.at[1],
        device_id=(across,),
        device_id_type=MESH,
    )
    own_copy = pltpu.make_async_copy(source, wide.at[pl.ds(0, count)], loads.at[0])
    sample_copy = pltpu.make_async_copy(sample, base, loads.at[1])
    list_copy = pltpu.make_async_copy(lists, index, loads.at[2])
    length_copy = pltpu.make_async_copy(lengths, counts, loads.at[3])
    own_copies = (own_copy, sample_copy, list_copy, length_copy)

    def fetch(box):
        return pltpu.make_async_copy(blocks.at[box], held.at[box], arrivals.at[box])

    barrier = pltpu.get_barrier_semaphore()
    pl.semaphore_signal(barrier, inc=1, device_id=(partner,), device_id_type=MESH)

    @pl.when(inside)
    def _():
        pl.semaphore_signal(barrier, inc=1, device_id=(across,), device_id_type=MESH)
        pl.semaphore_wait(barrier, 2)
        far_copy.start()

    @pl.when(jnp.logical_not(inside))
    def _():
        pl.semaphore_wait(barrier, 1)

    near_copy.start()
    for copy in own_copies:
        copy.start()
    for box in range(count):
        fetch(box).start()
    for copy in own_copies:
        copy.wait()
    near_copy.wait()

    def near(box, carry):
        fetch(box).wait()
        picked = []
        for slot in range(slots):
            place = index[slot, box] - me * count
            other = place - (1 - 2 * core) * count
            own = (place >= 0) & (place < count)
            beside = (other >= 0) & (other < count)
            pick = jnp.where(own, place, jnp.where(beside, other + count, 0))
            keep = ((own | beside) & (slot < counts[box])).astype(jnp.float32)
            picked.append(wide[pick] * keep.astype(jnp.bfloat16))
        part[box] = base[box].astype(jnp.float32) - jnp.dot(
            jnp.concatenate([held[box, slot] for slot in range(slots)], axis=1),
            jnp.concatenate(picked, axis=0),
            preferred_element_type=jnp.float32,
        )
        return carry

    lax.fori_loop(0, count, near, 0)

    @pl.when(inside)
    def _():
        far_copy.wait()


def halo_call(index, counts, source, blocks, sample):
    count, rows, samples = sample.shape
    anywhere = pl.BlockSpec(memory_space=pl.ANY)
    fixed = pl.BlockSpec(memory_space=pltpu.HBM)
    vmem = pl.BlockSpec(memory_space=pltpu.VMEM)
    return pl.pallas_call(
        halo_kernel,
        in_specs=[fixed] * 5,
        out_specs=[vmem, anywhere, vmem],
        out_shape=[
            jax.ShapeDtypeStruct(sample.shape, jnp.float32),
            jax.ShapeDtypeStruct(sample.shape, jnp.bfloat16),
            jax.ShapeDtypeStruct(blocks.shape, jnp.bfloat16),
        ],
        scratch_shapes=[
            pltpu.VMEM((2 * count, rows, samples), jnp.bfloat16),
            pltpu.VMEM((count, rows, samples), jnp.bfloat16),
            pltpu.SMEM(index.shape, jnp.int32),
            pltpu.SMEM(counts.shape, jnp.int32),
            pltpu.SemaphoreType.DMA((4,)),
            pltpu.SemaphoreType.DMA((count,)),
            pltpu.SemaphoreType.DMA((2,)),
            pltpu.SemaphoreType.DMA((2,)),
        ],
        compiler_params=pltpu.CompilerParams(
            collective_id=0, has_side_effects=True, vmem_limit_bytes=30 * 2**20
        ),
        name="halo",
    )(index, counts, source, blocks, sample)


def gram_kernel(
    index, counts, part, source, halo, blocks, start, moment, compact, far, picks
):
    count, rows, samples = far.shape
    slots = blocks.shape[1]
    half = samples // 2
    me = lax.axis_index(AXIS)
    core = lax.rem(me, 2)
    base = (me - 1 + 2 * core) * count

    found = jnp.int32(0)
    for box in range(count):
        far[box] = part[box]
        for slot in range(1, slots):
            place = index[slot, box] - base
            needed = (place >= 0) & (place < count) & (slot < counts[box])
            picks[found] = (box * slots + slot) * count + place
            found = found + needed.astype(jnp.int32)
    group = 4

    def multiply(turn, carry):
        terms = []
        for member in range(group):
            entry = turn * group + member
            code = picks[jnp.minimum(entry, found - 1)]
            block = lax.div(code, count)
            box = lax.div(block, slots)
            keep = (entry < found).astype(jnp.float32).astype(jnp.bfloat16)
            terms.append(
                (
                    box,
                    jnp.dot(
                        blocks[box, lax.rem(block, slots)],
                        halo[lax.rem(code, count)] * keep,
                        preferred_element_type=jnp.float32,
                    ),
                )
            )
        for box, term in terms:
            far[box] -= term
        return carry

    lax.fori_loop(0, lax.div(found + group - 1, group), multiply, 0)

    lanes_rows = lax.broadcasted_iota(jnp.int32, (rows, samples), 1)
    lanes = lax.broadcasted_iota(jnp.int32, (half, samples), 1)
    diagonal = lanes - half == lax.broadcasted_iota(jnp.int32, (half, samples), 0)
    together = 4 if count % 4 == 0 else 1

    def reduce(turn, carry):
        for member in range(together):
            box = turn * together + member
            value = far[box]
            doubled = value + pltpu.roll(value, half, 1)
            high = doubled.astype(jnp.bfloat16).astype(jnp.float32)
            both = jnp.where(lanes_rows < half, high, doubled - high).astype(jnp.bfloat16)
            compact[box] = both
            product = jnp.dot(
                both.T,
                jnp.concatenate([source[box], both], axis=1),
                preferred_element_type=jnp.float32,
            )
            moment[box] = product[:half, :samples] + product[half:, :samples]
            mixed = product[:half, samples:] + product[half:, samples:]
            start[box] = jnp.where(
                lanes < half, mixed + pltpu.roll(mixed, half, 1), diagonal.astype(jnp.float32)
            )
        return carry

    lax.fori_loop(0, count // together, reduce, 0)


def gram_call(index, counts, part, source, halo, blocks):
    count, rows, samples = part.shape
    slots = blocks.shape[1]
    half = samples // 2
    most = count * (slots - 1)
    smem = pl.BlockSpec(memory_space=pltpu.SMEM)
    vmem = pl.BlockSpec(memory_space=pltpu.VMEM)
    return pl.pallas_call(
        gram_kernel,
        in_specs=[smem, smem, vmem, vmem, vmem, vmem],
        out_specs=[vmem] * 3,
        out_shape=[
            jax.ShapeDtypeStruct((count, half, samples), jnp.float32),
            jax.ShapeDtypeStruct((count, half, samples), jnp.float32),
            jax.ShapeDtypeStruct((count, rows, samples), jnp.bfloat16),
        ],
        scratch_shapes=[
            pltpu.VMEM((count, rows, samples), jnp.float32),
            pltpu.SMEM((most + 1,), jnp.int32),
        ],
        compiler_params=pltpu.CompilerParams(vmem_limit_bytes=12 * 2**20),
        name="gram",
    )(index, counts, part, source, halo, blocks)


def factor(work, nodes, low, high, width):
    half, samples = work.shape[1:]
    octets = half // 8
    row8 = lax.broadcasted_iota(jnp.int32, (nodes, 8, samples), 1)

    def spread_row(value, row):
        return jnp.broadcast_to(value[:, row : row + 1, :], value.shape)

    def spread_column(value, lane):
        flat = value.reshape(nodes * 8, samples)
        return jnp.broadcast_to(flat[:, lane : lane + 1], flat.shape).reshape(value.shape)

    for place in range(low, high):
        base = 8 * place
        head = work[:nodes, base : base + 8, :]
        pivots = None
        for begin in range(0, 8, width):
            rows = range(begin, begin + width)
            columns = {row: spread_column(head, base + row) for row in rows}
            for row in rows:
                pivot = spread_row(columns[row], row)
                pivots = pivot if pivots is None else jnp.where(row8 >= row, pivot, pivots)
                if row == 7:
                    break
                scaled = jnp.where(row8 > row, columns[row] * (1.0 / pivot), 0.0)
                head = head - scaled * spread_row(head, row)
                for later in range(row + 1, begin + width):
                    columns[later] = columns[later] - scaled * spread_row(columns[later], row)
        root = head * lax.rsqrt(pivots)
        work[:nodes, base : base + 8, :] = root
        if place + 1 == octets:
            break
        high_part = root.astype(jnp.bfloat16).astype(jnp.float32)
        rest = root - high_part
        middle = rest.astype(jnp.bfloat16).astype(jnp.float32)
        low_part = rest - middle
        for node in range(nodes):
            h, m, t = high_part[node], middle[node], low_part[node]
            left = jnp.concatenate([h, h, m, m, h, t], axis=0).astype(jnp.bfloat16)
            right = jnp.concatenate([h, m, h, m, t, h], axis=0).astype(jnp.bfloat16)
            update = lax.dot_general(
                left[:, :half],
                right,
                (((0,), (0,)), ((), ())),
                preferred_element_type=jnp.float32,
            )
            work[node, base + 8 :, :] = work[node, base + 8 :, :] - update[base + 8 :, :]


def solved(matrix, right):
    half = right.shape[0]
    blank = jnp.zeros_like(right)
    middle = fine_dot(matrix, jnp.concatenate([blank, right], axis=0))
    return fine_dot(matrix, middle, ((0,), (0,)))[half:]


def packed(gram, moment):
    rows = gram.shape[0] // 2
    half = gram.shape[1] // 2
    lanes = lax.broadcasted_iota(jnp.int32, (rows, 2 * half), 1)
    top = jnp.where(lanes < half, gram[:rows], pltpu.roll(gram[rows:], half, 1))
    return jnp.concatenate([top, moment], axis=0)


def unpacked(value, half):
    rows = half // 2
    lanes = lax.broadcasted_iota(jnp.int32, (half, 2 * half), 1)
    diagonal = lanes - half == lax.broadcasted_iota(jnp.int32, (half, 2 * half), 0)
    gram = jnp.concatenate([value[:rows], pltpu.roll(value[:rows], half, 1)], axis=0)
    return jnp.where(lanes < half, gram, diagonal.astype(jnp.float32))


def tree_kernel(spread, start, moment, work, answers, sums, arrived, sent, landed):
    count, half, samples = start.shape
    depth = count.bit_length() - 1
    me = lax.axis_index(AXIS)
    bits = [lax.rem(lax.div(me, 1 << step), 2) for step in range(spread)]
    partners = [me + (1 - 2 * bit) * (1 << step) for step, bit in enumerate(bits)]
    barrier = pltpu.get_barrier_semaphore()
    for partner in partners:
        pl.semaphore_signal(barrier, inc=1, device_id=(partner,), device_id_type=MESH)

    chunks = sent.shape[1]
    size = sums.shape[1] // chunks

    def exchange(step, chunk):
        part = pl.ds(chunk * size, size)
        return pltpu.make_async_remote_copy(
            src_ref=sums.at[step, part],
            dst_ref=arrived.at[step, part],
            send_sem=sent.at[step, chunk],
            recv_sem=landed.at[step, chunk],
            device_id=(partners[step],),
            device_id_type=MESH,
        )

    grams = {(0, leaf): start[leaf] for leaf in range(count)}
    moments = {(0, leaf): moment[leaf] for leaf in range(count)}
    for height in range(1, depth + 1):
        for node in range(count >> height):
            for table in (grams, moments):
                table[height, node] = (
                    table[height - 1, 2 * node] + table[height - 1, 2 * node + 1]
                )
    sums[0] = packed(grams[depth, 0], moments[depth, 0])
    pl.semaphore_wait(barrier, spread)
    for chunk in range(chunks):
        exchange(0, chunk).start()

    lanes = lax.broadcasted_iota(jnp.int32, (half, samples), 1)
    diagonal = lanes - half == lax.broadcasted_iota(jnp.int32, (half, samples), 0)
    for leaf in range(count):
        work[leaf] = start[leaf]
    place = count
    targets = [(leaf, moments[0, leaf]) for leaf in range(count)]
    for height in range(1, depth + 1):
        targets.append((place, moments[height, 0]))
        for side in range(1 if height == depth else 2):
            work[place] = jnp.where(
                lanes < half, grams[height, side], diagonal.astype(jnp.float32)
            )
            place += 1
    octets = half // 8
    turns = max(spread - 1, 1)
    for step in range(spread):
        if step < turns:
            factor(work, place, octets * step // turns, octets * (step + 1) // turns, 4)
        if step == spread - 1:
            for row, (node, right) in enumerate(targets):
                answers[row] = solved(work[node], right)
        for chunk in range(chunks):
            part = pl.ds(chunk * size, size)
            exchange(step, chunk).wait_recv()
            sums[step + 1, part] = sums[step, part] + arrived[step, part]
            if step + 1 < spread:
                exchange(step + 1, chunk).start()
    for step in range(spread):
        for chunk in range(chunks):
            exchange(step, chunk).wait_send()


def tree_call(start, moment, spread):
    count, half, samples = start.shape
    depth = count.bit_length() - 1
    nodes = count + 2 * depth - 1
    rows = half // 2 + half
    vmem = pl.BlockSpec(memory_space=pltpu.VMEM)
    return pl.pallas_call(
        functools.partial(tree_kernel, spread),
        in_specs=[vmem] * 2,
        out_specs=[vmem] * 4,
        out_shape=[
            jax.ShapeDtypeStruct((nodes, half, samples), jnp.float32),
            jax.ShapeDtypeStruct((count + depth, half, samples), jnp.float32),
            jax.ShapeDtypeStruct((spread + 1, rows, samples), jnp.float32),
            jax.ShapeDtypeStruct((spread, rows, samples), jnp.float32),
        ],
        scratch_shapes=[
            pltpu.SemaphoreType.DMA((spread, 3)),
            pltpu.SemaphoreType.DMA((spread, 3)),
        ],
        compiler_params=pltpu.CompilerParams(
            collective_id=1, has_side_effects=True, vmem_limit_bytes=12 * 2**20
        ),
        name="tree",
    )(start, moment)


def out_kernel(
    work, answers, sums, arrived, compact, leaf_out, level_out, tops, leaves, sems
):
    count, rows, samples = compact.shape
    half = answers.shape[1]
    depth = count.bit_length() - 1
    spread = arrived.shape[0]
    me = lax.axis_index(AXIS)
    lanes = lax.broadcasted_iota(jnp.int32, (half, samples), 1)
    triangle = lanes >= lax.broadcasted_iota(jnp.int32, (half, samples), 0)
    corner = triangle & (lanes < half)
    blank = jnp.zeros((half, samples), jnp.float32)

    def sketch(one, two, answer):
        stacked = jnp.concatenate(
            [jnp.where(corner, one, 0.0), jnp.where(corner, two, 0.0)], axis=0
        )
        return fine_dot(stacked, jnp.concatenate([answer, blank], axis=0))

    for step in range(spread):
        tops[2 * step] = unpacked(arrived[step], half)
        tops[2 * step + 1] = unpacked(sums[step + 1], half)
    octets = half // 8
    copies = []
    for turn in range(octets):
        factor(tops, 2 * spread, turn, turn + 1, 8)
        first, last = count * turn // octets, count * (turn + 1) // octets
        for leaf in range(first, last):
            answer = answers[leaf]
            high = answer.astype(jnp.bfloat16)
            low = (answer - high.astype(jnp.float32)).astype(jnp.bfloat16)
            pair = jnp.concatenate([high, low], axis=1)
            both = jnp.dot(
                compact[leaf],
                jnp.concatenate([pair, pair], axis=0),
                preferred_element_type=jnp.float32,
            )
            leaves[leaf] = (both[:, :samples] + both[:, samples:]).astype(leaves.dtype)
        if last > first:
            part = pl.ds(first, last - first)
            copy = pltpu.make_async_copy(leaves.at[part], leaf_out.at[part], sems.at[turn])
            copy.start()
            copies.append(copy)
    for height in range(1, depth + 1):
        first = 0 if height == 1 else count + 2 * (height - 2)
        level_out[0, height - 1] = sketch(
            work[first], work[first + 1], answers[count + height - 1]
        ).astype(level_out.dtype)
    for step in range(spread):
        mine = work[count + 2 * (depth - 1)] if step == 0 else tops[2 * step - 1]
        other = tops[2 * step]
        odd = lax.rem(lax.div(me, 1 << step), 2) == 1
        answer = solved(tops[2 * step + 1], sums[step + 1, half // 2 :, :])
        level_out[0, depth + step] = sketch(
            jnp.where(odd, other, mine), jnp.where(odd, mine, other), answer
        ).astype(level_out.dtype)
    for copy in copies:
        copy.wait()


def out_call(work, answers, sums, arrived, compact):
    count, rows, samples = compact.shape
    half = answers.shape[1]
    spread = arrived.shape[0]
    depth = count.bit_length() - 1
    vmem = pl.BlockSpec(memory_space=pltpu.VMEM)
    return pl.pallas_call(
        out_kernel,
        in_specs=[vmem] * 5,
        out_specs=[pl.BlockSpec(memory_space=pl.ANY), vmem],
        out_shape=[
            jax.ShapeDtypeStruct((count, rows, samples), jnp.bfloat16),
            jax.ShapeDtypeStruct((1, depth + spread, samples, samples), jnp.bfloat16),
        ],
        scratch_shapes=[
            pltpu.VMEM((2 * spread, half, samples), jnp.float32),
            pltpu.VMEM((count, rows, samples), jnp.bfloat16),
            pltpu.SemaphoreType.DMA((half // 8,)),
        ],
        compiler_params=pltpu.CompilerParams(vmem_limit_bytes=12 * 2**20),
        name="out",
    )(work, answers, sums, arrived, compact)


def per_device(random_block, sample_block, near_blocks, near_index, near_count):
    spread = lax.axis_size(AXIS).bit_length() - 1
    index = near_index.T
    fixed = [
        pltpu.with_memory_space_constraint(value, pltpu.HBM)
        for value in (index, near_count, random_block, near_blocks, sample_block)
    ]
    part, halo, held = halo_call(*fixed)
    start, moment, compact = gram_call(
        index, near_count, part, random_block, halo, held
    )
    work, answers, sums, arrived = tree_call(start, moment, spread)
    return tuple(out_call(work, answers, sums, arrived, compact))


def solution(mesh):
    return jax.shard_map(
        per_device,
        mesh=mesh,
        in_specs=(
            P(AXIS, None, None),
            P(AXIS, None, None),
            P(AXIS, None, None, None),
            P(AXIS, None),
            P(AXIS),
        ),
        out_specs=(P(AXIS, None, None), P(AXIS, None, None, None)),
        check_vma=False,
    )
```

```python
import functools

import jax
import jax.numpy as jnp
from jax import lax
from jax.experimental import pallas as pl
from jax.experimental.pallas import tpu as pltpu
from jax.sharding import PartitionSpec as P

AXIS = "boxes"
MESH = pl.DeviceIdType.MESH


def fine_dot(a, b, dims=((1,), (0,))):
    return lax.dot_general(
        a, b, (dims, ((), ())), precision=lax.Precision.HIGH, preferred_element_type=jnp.float32
    )


def halo_kernel(
    lists,
    lengths,
    source,
    blocks,
    sample,
    part,
    halo,
    held,
    wide,
    base,
    index,
    counts,
    loads,
    arrivals,
    sent,
    landed,
):
    count, slots, rows = held.shape[:3]
    samples = part.shape[2]
    size = lax.axis_size(AXIS)
    me = lax.axis_index(AXIS)
    core = lax.rem(me, 2)
    partner = me + 1 - 2 * core
    across = me - 1 + 2 * core
    inside = (across >= 0) & (across < size)
    near_copy = pltpu.make_async_remote_copy(
        src_ref=source,
        dst_ref=wide.at[pl.ds(count, count)],
        send_sem=sent.at[0],
        recv_sem=landed.at[0],
        device_id=(partner,),
        device_id_type=MESH,
    )
    far_copy = pltpu.make_async_remote_copy(
        src_ref=source,
        dst_ref=halo,
        send_sem=sent.at[1],
        recv_sem=landed.at[1],
        device_id=(across,),
        device_id_type=MESH,
    )
    own_copy = pltpu.make_async_copy(source, wide.at[pl.ds(0, count)], loads.at[0])
    sample_copy = pltpu.make_async_copy(sample, base, loads.at[1])
    list_copy = pltpu.make_async_copy(lists, index, loads.at[2])
    length_copy = pltpu.make_async_copy(lengths, counts, loads.at[3])
    own_copies = (own_copy, sample_copy, list_copy, length_copy)

    def fetch(box):
        return pltpu.make_async_copy(blocks.at[box], held.at[box], arrivals.at[box])

    barrier = pltpu.get_barrier_semaphore()
    pl.semaphore_signal(barrier, inc=1, device_id=(partner,), device_id_type=MESH)

    @pl.when(inside)
    def _():
        pl.semaphore_signal(barrier, inc=1, device_id=(across,), device_id_type=MESH)
        pl.semaphore_wait(barrier, 2)
        far_copy.start()

    @pl.when(jnp.logical_not(inside))
    def _():
        pl.semaphore_wait(barrier, 1)

    near_copy.start()
    for copy in own_copies:
        copy.start()
    for box in range(count):
        fetch(box).start()
    for copy in own_copies:
        copy.wait()
    near_copy.wait()

    def near(box, carry):
        fetch(box).wait()
        picked = []
        for slot in range(slots):
            place = index[slot, box] - me * count
            other = place - (1 - 2 * core) * count
            own = (place >= 0) & (place < count)
            beside = (other >= 0) & (other < count)
            pick = jnp.where(own, place, jnp.where(beside, other + count, 0))
            keep = ((own | beside) & (slot < counts[box])).astype(jnp.float32)
            picked.append(wide[pick] * keep.astype(jnp.bfloat16))
        part[box] = base[box].astype(jnp.float32) - jnp.dot(
            jnp.concatenate([held[box, slot] for slot in range(slots)], axis=1),
            jnp.concatenate(picked, axis=0),
            preferred_element_type=jnp.float32,
        )
        return carry

    lax.fori_loop(0, count, near, 0)

    @pl.when(inside)
    def _():
        far_copy.wait()


def halo_call(index, counts, source, blocks, sample):
    count, rows, samples = sample.shape
    anywhere = pl.BlockSpec(memory_space=pl.ANY)
    fixed = pl.BlockSpec(memory_space=pltpu.HBM)
    vmem = pl.BlockSpec(memory_space=pltpu.VMEM)
    return pl.pallas_call(
        halo_kernel,
        in_specs=[fixed] * 5,
        out_specs=[vmem, anywhere, vmem],
        out_shape=[
            jax.ShapeDtypeStruct(sample.shape, jnp.float32),
            jax.ShapeDtypeStruct(sample.shape, jnp.bfloat16),
            jax.ShapeDtypeStruct(blocks.shape, jnp.bfloat16),
        ],
        scratch_shapes=[
            pltpu.VMEM((2 * count, rows, samples), jnp.bfloat16),
            pltpu.VMEM((count, rows, samples), jnp.bfloat16),
            pltpu.SMEM(index.shape, jnp.int32),
            pltpu.SMEM(counts.shape, jnp.int32),
            pltpu.SemaphoreType.DMA((4,)),
            pltpu.SemaphoreType.DMA((count,)),
            pltpu.SemaphoreType.DMA((2,)),
            pltpu.SemaphoreType.DMA((2,)),
        ],
        compiler_params=pltpu.CompilerParams(
            collective_id=0, has_side_effects=True, vmem_limit_bytes=30 * 2**20
        ),
        name="halo",
    )(index, counts, source, blocks, sample)


def gram_kernel(
    index, counts, part, source, halo, blocks, start, moment, compact, far, picks
):
    count, rows, samples = far.shape
    slots = blocks.shape[1]
    half = samples // 2
    me = lax.axis_index(AXIS)
    core = lax.rem(me, 2)
    base = (me - 1 + 2 * core) * count

    found = jnp.int32(0)
    for box in range(count):
        far[box] = part[box]
        for slot in range(1, slots):
            place = index[slot, box] - base
            needed = (place >= 0) & (place < count) & (slot < counts[box])
            picks[found] = (box * slots + slot) * count + place
            found = found + needed.astype(jnp.int32)
    group = 4

    def multiply(turn, carry):
        terms = []
        for member in range(group):
            entry = turn * group + member
            code = picks[jnp.minimum(entry, found - 1)]
            block = lax.div(code, count)
            box = lax.div(block, slots)
            keep = (entry < found).astype(jnp.float32).astype(jnp.bfloat16)
            terms.append(
                (
                    box,
                    jnp.dot(
                        blocks[box, lax.rem(block, slots)],
                        halo[lax.rem(code, count)] * keep,
                        preferred_element_type=jnp.float32,
                    ),
                )
            )
        for box, term in terms:
            far[box] -= term
        return carry

    lax.fori_loop(0, lax.div(found + group - 1, group), multiply, 0)

    lanes_rows = lax.broadcasted_iota(jnp.int32, (rows, samples), 1)
    lanes = lax.broadcasted_iota(jnp.int32, (half, samples), 1)
    diagonal = lanes - half == lax.broadcasted_iota(jnp.int32, (half, samples), 0)
    together = 4 if count % 4 == 0 else 1

    def reduce(turn, carry):
        for member in range(together):
            box = turn * together + member
            value = far[box]
            doubled = value + pltpu.roll(value, half, 1)
            high = doubled.astype(jnp.bfloat16).astype(jnp.float32)
            both = jnp.where(lanes_rows < half, high, doubled - high).astype(jnp.bfloat16)
            compact[box] = both
            product = jnp.dot(
                both.T,
                jnp.concatenate([source[box], both], axis=1),
                preferred_element_type=jnp.float32,
            )
            moment[box] = product[:half, :samples] + product[half:, :samples]
            mixed = product[:half, samples:] + product[half:, samples:]
            start[box] = jnp.where(
                lanes < half, mixed + pltpu.roll(mixed, half, 1), diagonal.astype(jnp.float32)
            )
        return carry

    lax.fori_loop(0, count // together, reduce, 0)


def gram_call(index, counts, part, source, halo, blocks):
    count, rows, samples = part.shape
    slots = blocks.shape[1]
    half = samples // 2
    most = count * (slots - 1)
    smem = pl.BlockSpec(memory_space=pltpu.SMEM)
    vmem = pl.BlockSpec(memory_space=pltpu.VMEM)
    return pl.pallas_call(
        gram_kernel,
        in_specs=[smem, smem, vmem, vmem, vmem, vmem],
        out_specs=[vmem] * 3,
        out_shape=[
            jax.ShapeDtypeStruct((count, half, samples), jnp.float32),
            jax.ShapeDtypeStruct((count, half, samples), jnp.float32),
            jax.ShapeDtypeStruct((count, rows, samples), jnp.bfloat16),
        ],
        scratch_shapes=[
            pltpu.VMEM((count, rows, samples), jnp.float32),
            pltpu.SMEM((most + 1,), jnp.int32),
        ],
        compiler_params=pltpu.CompilerParams(vmem_limit_bytes=12 * 2**20),
        name="gram",
    )(index, counts, part, source, halo, blocks)


def factor(work, nodes, low, high, width):
    half, samples = work.shape[1:]
    octets = half // 8
    row8 = lax.broadcasted_iota(jnp.int32, (nodes, 8, samples), 1)

    def spread_row(value, row):
        return jnp.broadcast_to(value[:, row : row + 1, :], value.shape)

    def spread_column(value, lane):
        flat = value.reshape(nodes * 8, samples)
        return jnp.broadcast_to(flat[:, lane : lane + 1], flat.shape).reshape(value.shape)

    for place in range(low, high):
        base = 8 * place
        head = work[:nodes, base : base + 8, :]
        pivots = None
        for begin in range(0, 8, width):
            rows = range(begin, begin + width)
            columns = {row: spread_column(head, base + row) for row in rows}
            for row in rows:
                pivot = spread_row(columns[row], row)
                pivots = pivot if pivots is None else jnp.where(row8 >= row, pivot, pivots)
                if row == 7:
                    break
                scaled = jnp.where(row8 > row, columns[row] * (1.0 / pivot), 0.0)
                head = head - scaled * spread_row(head, row)
                for later in range(row + 1, begin + width):
                    columns[later] = columns[later] - scaled * spread_row(columns[later], row)
        root = head * lax.rsqrt(pivots)
        work[:nodes, base : base + 8, :] = root
        if place + 1 == octets:
            break
        high_part = root.astype(jnp.bfloat16).astype(jnp.float32)
        rest = root - high_part
        middle = rest.astype(jnp.bfloat16).astype(jnp.float32)
        low_part = rest - middle
        for node in range(nodes):
            h, m, t = high_part[node], middle[node], low_part[node]
            left = jnp.concatenate([h, h, m, m, h, t], axis=0).astype(jnp.bfloat16)
            right = jnp.concatenate([h, m, h, m, t, h], axis=0).astype(jnp.bfloat16)
            update = lax.dot_general(
                left[:, :half],
                right,
                (((0,), (0,)), ((), ())),
                preferred_element_type=jnp.float32,
            )
            work[node, base + 8 :, :] = work[node, base + 8 :, :] - update[base + 8 :, :]


def solved(matrix, right):
    half = right.shape[0]
    blank = jnp.zeros_like(right)
    middle = fine_dot(matrix, jnp.concatenate([blank, right], axis=0))
    return fine_dot(matrix, middle, ((0,), (0,)))[half:]


def packed(gram, moment):
    rows = gram.shape[0] // 2
    half = gram.shape[1] // 2
    lanes = lax.broadcasted_iota(jnp.int32, (rows, 2 * half), 1)
    top = jnp.where(lanes < half, gram[:rows], pltpu.roll(gram[rows:], half, 1))
    return jnp.concatenate([top, moment], axis=0)


def unpacked(value, half):
    rows = half // 2
    lanes = lax.broadcasted_iota(jnp.int32, (half, 2 * half), 1)
    diagonal = lanes - half == lax.broadcasted_iota(jnp.int32, (half, 2 * half), 0)
    gram = jnp.concatenate([value[:rows], pltpu.roll(value[:rows], half, 1)], axis=0)
    return jnp.where(lanes < half, gram, diagonal.astype(jnp.float32))


def tree_kernel(spread, start, moment, work, answers, sums, arrived, sent, landed):
    count, half, samples = start.shape
    depth = count.bit_length() - 1
    me = lax.axis_index(AXIS)
    bits = [lax.rem(lax.div(me, 1 << step), 2) for step in range(spread)]
    partners = [me + (1 - 2 * bit) * (1 << step) for step, bit in enumerate(bits)]
    barrier = pltpu.get_barrier_semaphore()
    for partner in partners:
        pl.semaphore_signal(barrier, inc=1, device_id=(partner,), device_id_type=MESH)

    chunks = sent.shape[1]
    size = sums.shape[1] // chunks

    def exchange(step, chunk):
        part = pl.ds(chunk * size, size)
        return pltpu.make_async_remote_copy(
            src_ref=sums.at[step, part],
            dst_ref=arrived.at[step, part],
            send_sem=sent.at[step, chunk],
            recv_sem=landed.at[step, chunk],
            device_id=(partners[step],),
            device_id_type=MESH,
        )

    grams = {(0, leaf): start[leaf] for leaf in range(count)}
    moments = {(0, leaf): moment[leaf] for leaf in range(count)}
    for height in range(1, depth + 1):
        for node in range(count >> height):
            for table in (grams, moments):
                table[height, node] = (
                    table[height - 1, 2 * node] + table[height - 1, 2 * node + 1]
                )
    sums[0] = packed(grams[depth, 0], moments[depth, 0])
    pl.semaphore_wait(barrier, spread)
    for chunk in range(chunks):
        exchange(0, chunk).start()

    lanes = lax.broadcasted_iota(jnp.int32, (half, samples), 1)
    diagonal = lanes - half == lax.broadcasted_iota(jnp.int32, (half, samples), 0)
    for leaf in range(count):
        work[leaf] = start[leaf]
    place = count
    targets = [(leaf, moments[0, leaf]) for leaf in range(count)]
    for height in range(1, depth + 1):
        targets.append((place, moments[height, 0]))
        for side in range(1 if height == depth else 2):
            work[place] = jnp.where(
                lanes < half, grams[height, side], diagonal.astype(jnp.float32)
            )
            place += 1
    octets = half // 8
    turns = max(spread - 2, 1)
    begin = min(turns, spread - 1)
    for step in range(spread):
        if step < turns:
            factor(work, place, octets * step // turns, octets * (step + 1) // turns, 4)
        if step >= begin:
            some = len(targets) * (step - begin) // (spread - begin)
            more = len(targets) * (step - begin + 1) // (spread - begin)
            for row in range(some, more):
                node, right = targets[row]
                answers[row] = solved(work[node], right)
        for chunk in range(chunks):
            part = pl.ds(chunk * size, size)
            exchange(step, chunk).wait_recv()
            sums[step + 1, part] = sums[step, part] + arrived[step, part]
            if step + 1 < spread:
                exchange(step + 1, chunk).start()
    for step in range(spread):
        for chunk in range(chunks):
            exchange(step, chunk).wait_send()


def tree_call(start, moment, spread):
    count, half, samples = start.shape
    depth = count.bit_length() - 1
    nodes = count + 2 * depth - 1
    rows = half // 2 + half
    vmem = pl.BlockSpec(memory_space=pltpu.VMEM)
    return pl.pallas_call(
        functools.partial(tree_kernel, spread),
        in_specs=[vmem] * 2,
        out_specs=[vmem] * 4,
        out_shape=[
            jax.ShapeDtypeStruct((nodes, half, samples), jnp.float32),
            jax.ShapeDtypeStruct((count + depth, half, samples), jnp.float32),
            jax.ShapeDtypeStruct((spread + 1, rows, samples), jnp.float32),
            jax.ShapeDtypeStruct((spread, rows, samples), jnp.float32),
        ],
        scratch_shapes=[
            pltpu.SemaphoreType.DMA((spread, 3)),
            pltpu.SemaphoreType.DMA((spread, 3)),
        ],
        compiler_params=pltpu.CompilerParams(
            collective_id=1, has_side_effects=True, vmem_limit_bytes=12 * 2**20
        ),
        name="tree",
    )(start, moment)


def out_kernel(
    work, answers, sums, arrived, compact, leaf_out, level_out, tops, leaves, sems
):
    count, rows, samples = compact.shape
    half = answers.shape[1]
    depth = count.bit_length() - 1
    spread = arrived.shape[0]
    me = lax.axis_index(AXIS)
    lanes = lax.broadcasted_iota(jnp.int32, (half, samples), 1)
    triangle = lanes >= lax.broadcasted_iota(jnp.int32, (half, samples), 0)
    corner = triangle & (lanes < half)
    blank = jnp.zeros((half, samples), jnp.float32)

    def sketch(one, two, answer):
        stacked = jnp.concatenate(
            [jnp.where(corner, one, 0.0), jnp.where(corner, two, 0.0)], axis=0
        )
        return fine_dot(stacked, jnp.concatenate([answer, blank], axis=0))

    for step in range(spread):
        tops[2 * step] = unpacked(arrived[step], half)
        tops[2 * step + 1] = unpacked(sums[step + 1], half)
    octets = half // 8
    copies = []
    for turn in range(octets):
        factor(tops, 2 * spread, turn, turn + 1, 8)
        first, last = count * turn // octets, count * (turn + 1) // octets
        for leaf in range(first, last):
            answer = answers[leaf]
            high = answer.astype(jnp.bfloat16)
            low = (answer - high.astype(jnp.float32)).astype(jnp.bfloat16)
            pair = jnp.concatenate([high, low], axis=1)
            both = jnp.dot(
                compact[leaf],
                jnp.concatenate([pair, pair], axis=0),
                preferred_element_type=jnp.float32,
            )
            leaves[leaf] = (both[:, :samples] + both[:, samples:]).astype(leaves.dtype)
        if last > first:
            part = pl.ds(first, last - first)
            copy = pltpu.make_async_copy(leaves.at[part], leaf_out.at[part], sems.at[turn])
            copy.start()
            copies.append(copy)
    for height in range(1, depth + 1):
        first = 0 if height == 1 else count + 2 * (height - 2)
        level_out[0, height - 1] = sketch(
            work[first], work[first + 1], answers[count + height - 1]
        ).astype(level_out.dtype)
    for step in range(spread):
        mine = work[count + 2 * (depth - 1)] if step == 0 else tops[2 * step - 1]
        other = tops[2 * step]
        odd = lax.rem(lax.div(me, 1 << step), 2) == 1
        answer = solved(tops[2 * step + 1], sums[step + 1, half // 2 :, :])
        level_out[0, depth + step] = sketch(
            jnp.where(odd, other, mine), jnp.where(odd, mine, other), answer
        ).astype(level_out.dtype)
    for copy in copies:
        copy.wait()


def out_call(work, answers, sums, arrived, compact):
    count, rows, samples = compact.shape
    half = answers.shape[1]
    spread = arrived.shape[0]
    depth = count.bit_length() - 1
    vmem = pl.BlockSpec(memory_space=pltpu.VMEM)
    return pl.pallas_call(
        out_kernel,
        in_specs=[vmem] * 5,
        out_specs=[pl.BlockSpec(memory_space=pl.ANY), vmem],
        out_shape=[
            jax.ShapeDtypeStruct((count, rows, samples), jnp.bfloat16),
            jax.ShapeDtypeStruct((1, depth + spread, samples, samples), jnp.bfloat16),
        ],
        scratch_shapes=[
            pltpu.VMEM((2 * spread, half, samples), jnp.float32),
            pltpu.VMEM((count, rows, samples), jnp.bfloat16),
            pltpu.SemaphoreType.DMA((half // 8,)),
        ],
        compiler_params=pltpu.CompilerParams(vmem_limit_bytes=12 * 2**20),
        name="out",
    )(work, answers, sums, arrived, compact)


def per_device(random_block, sample_block, near_blocks, near_index, near_count):
    spread = lax.axis_size(AXIS).bit_length() - 1
    index = near_index.T
    fixed = [
        pltpu.with_memory_space_constraint(value, pltpu.HBM)
        for value in (index, near_count, random_block, near_blocks, sample_block)
    ]
    part, halo, held = halo_call(*fixed)
    start, moment, compact = gram_call(
        index, near_count, part, random_block, halo, held
    )
    work, answers, sums, arrived = tree_call(start, moment, spread)
    return tuple(out_call(work, answers, sums, arrived, compact))


def solution(mesh):
    return jax.shard_map(
        per_device,
        mesh=mesh,
        in_specs=(
            P(AXIS, None, None),
            P(AXIS, None, None),
            P(AXIS, None, None, None),
            P(AXIS, None),
            P(AXIS),
        ),
        out_specs=(P(AXIS, None, None), P(AXIS, None, None, None)),
        check_vma=False,
    )
```

```python
import functools

import jax
import jax.numpy as jnp
from jax import lax
from jax.experimental import pallas as pl
from jax.experimental.pallas import tpu as pltpu
from jax.sharding import PartitionSpec as P

AXIS = "boxes"
MESH = pl.DeviceIdType.MESH


def fine_dot(a, b, dims=((1,), (0,))):
    return lax.dot_general(
        a, b, (dims, ((), ())), precision=lax.Precision.HIGH, preferred_element_type=jnp.float32
    )


def halo_kernel(
    lists,
    lengths,
    source,
    blocks,
    sample,
    part,
    halo,
    held,
    wide,
    base,
    index,
    counts,
    loads,
    arrivals,
    sent,
    landed,
):
    count, slots, rows = held.shape[:3]
    samples = part.shape[2]
    size = lax.axis_size(AXIS)
    me = lax.axis_index(AXIS)
    core = lax.rem(me, 2)
    partner = me + 1 - 2 * core
    across = me - 1 + 2 * core
    inside = (across >= 0) & (across < size)
    near_copy = pltpu.make_async_remote_copy(
        src_ref=source,
        dst_ref=wide.at[pl.ds(count, count)],
        send_sem=sent.at[0],
        recv_sem=landed.at[0],
        device_id=(partner,),
        device_id_type=MESH,
    )
    far_copy = pltpu.make_async_remote_copy(
        src_ref=source,
        dst_ref=halo,
        send_sem=sent.at[1],
        recv_sem=landed.at[1],
        device_id=(across,),
        device_id_type=MESH,
    )
    own_copy = pltpu.make_async_copy(source, wide.at[pl.ds(0, count)], loads.at[0])
    sample_copy = pltpu.make_async_copy(sample, base, loads.at[1])
    list_copy = pltpu.make_async_copy(lists, index, loads.at[2])
    length_copy = pltpu.make_async_copy(lengths, counts, loads.at[3])
    own_copies = (own_copy, sample_copy, list_copy, length_copy)

    def fetch(box):
        return pltpu.make_async_copy(blocks.at[box], held.at[box], arrivals.at[box])

    barrier = pltpu.get_barrier_semaphore()
    pl.semaphore_signal(barrier, inc=1, device_id=(partner,), device_id_type=MESH)

    @pl.when(inside)
    def _():
        pl.semaphore_signal(barrier, inc=1, device_id=(across,), device_id_type=MESH)
        pl.semaphore_wait(barrier, 2)
        far_copy.start()

    @pl.when(jnp.logical_not(inside))
    def _():
        pl.semaphore_wait(barrier, 1)

    near_copy.start()
    for copy in own_copies:
        copy.start()
    for box in range(count):
        fetch(box).start()
    for copy in own_copies:
        copy.wait()
    near_copy.wait()

    def near(box, carry):
        fetch(box).wait()
        picked = []
        for slot in range(slots):
            place = index[slot, box] - me * count
            other = place - (1 - 2 * core) * count
            own = (place >= 0) & (place < count)
            beside = (other >= 0) & (other < count)
            pick = jnp.where(own, place, jnp.where(beside, other + count, 0))
            keep = ((own | beside) & (slot < counts[box])).astype(jnp.float32)
            picked.append(wide[pick] * keep.astype(jnp.bfloat16))
        part[box] = base[box].astype(jnp.float32) - jnp.dot(
            jnp.concatenate([held[box, slot] for slot in range(slots)], axis=1),
            jnp.concatenate(picked, axis=0),
            preferred_element_type=jnp.float32,
        )
        return carry

    lax.fori_loop(0, count, near, 0)

    @pl.when(inside)
    def _():
        far_copy.wait()


def halo_call(index, counts, source, blocks, sample):
    count, rows, samples = sample.shape
    anywhere = pl.BlockSpec(memory_space=pl.ANY)
    fixed = pl.BlockSpec(memory_space=pltpu.HBM)
    vmem = pl.BlockSpec(memory_space=pltpu.VMEM)
    return pl.pallas_call(
        halo_kernel,
        in_specs=[fixed] * 5,
        out_specs=[vmem, anywhere, vmem],
        out_shape=[
            jax.ShapeDtypeStruct(sample.shape, jnp.float32),
            jax.ShapeDtypeStruct(sample.shape, jnp.bfloat16),
            jax.ShapeDtypeStruct(blocks.shape, jnp.bfloat16),
        ],
        scratch_shapes=[
            pltpu.VMEM((2 * count, rows, samples), jnp.bfloat16),
            pltpu.VMEM((count, rows, samples), jnp.bfloat16),
            pltpu.SMEM(index.shape, jnp.int32),
            pltpu.SMEM(counts.shape, jnp.int32),
            pltpu.SemaphoreType.DMA((4,)),
            pltpu.SemaphoreType.DMA((count,)),
            pltpu.SemaphoreType.DMA((2,)),
            pltpu.SemaphoreType.DMA((2,)),
        ],
        compiler_params=pltpu.CompilerParams(
            collective_id=0, has_side_effects=True, vmem_limit_bytes=30 * 2**20
        ),
        name="halo",
    )(index, counts, source, blocks, sample)


def gram_kernel(
    index, counts, part, source, halo, blocks, start, moment, compact, far, picks
):
    count, rows, samples = far.shape
    slots = blocks.shape[1]
    half = samples // 2
    me = lax.axis_index(AXIS)
    core = lax.rem(me, 2)
    base = (me - 1 + 2 * core) * count

    found = jnp.int32(0)
    for box in range(count):
        far[box] = part[box]
        for slot in range(1, slots):
            place = index[slot, box] - base
            needed = (place >= 0) & (place < count) & (slot < counts[box])
            picks[found] = (box * slots + slot) * count + place
            found = found + needed.astype(jnp.int32)
    group = 8

    def multiply(turn, carry):
        for member in range(group):
            entry = turn * group + member
            code = picks[jnp.minimum(entry, found - 1)]
            block = lax.div(code, count)
            box = lax.div(block, slots)
            keep = (entry < found).astype(jnp.float32).astype(jnp.bfloat16)
            far[box] -= jnp.dot(
                blocks[box, lax.rem(block, slots)],
                halo[lax.rem(code, count)] * keep,
                preferred_element_type=jnp.float32,
            )
        return carry

    lax.fori_loop(0, lax.div(found + group - 1, group), multiply, 0)

    lanes_rows = lax.broadcasted_iota(jnp.int32, (rows, samples), 1)
    lanes = lax.broadcasted_iota(jnp.int32, (half, samples), 1)
    diagonal = lanes - half == lax.broadcasted_iota(jnp.int32, (half, samples), 0)
    together = 4 if count % 4 == 0 else 1

    def reduce(turn, carry):
        for member in range(together):
            box = turn * together + member
            value = far[box]
            doubled = value + pltpu.roll(value, half, 1)
            high = doubled.astype(jnp.bfloat16).astype(jnp.float32)
            both = jnp.where(lanes_rows < half, high, doubled - high).astype(jnp.bfloat16)
            compact[box] = both
            product = jnp.dot(
                both.T,
                jnp.concatenate([source[box], both], axis=1),
                preferred_element_type=jnp.float32,
            )
            moment[box] = product[:half, :samples] + product[half:, :samples]
            mixed = product[:half, samples:] + product[half:, samples:]
            start[box] = jnp.where(
                lanes < half, mixed + pltpu.roll(mixed, half, 1), diagonal.astype(jnp.float32)
            )
        return carry

    lax.fori_loop(0, count // together, reduce, 0)


def gram_call(index, counts, part, source, halo, blocks):
    count, rows, samples = part.shape
    slots = blocks.shape[1]
    half = samples // 2
    most = count * (slots - 1)
    smem = pl.BlockSpec(memory_space=pltpu.SMEM)
    vmem = pl.BlockSpec(memory_space=pltpu.VMEM)
    return pl.pallas_call(
        gram_kernel,
        in_specs=[smem, smem, vmem, vmem, vmem, vmem],
        out_specs=[vmem] * 3,
        out_shape=[
            jax.ShapeDtypeStruct((count, half, samples), jnp.float32),
            jax.ShapeDtypeStruct((count, half, samples), jnp.float32),
            jax.ShapeDtypeStruct((count, rows, samples), jnp.bfloat16),
        ],
        scratch_shapes=[
            pltpu.VMEM((count, rows, samples), jnp.float32),
            pltpu.SMEM((most + 1,), jnp.int32),
        ],
        compiler_params=pltpu.CompilerParams(vmem_limit_bytes=12 * 2**20),
        name="gram",
    )(index, counts, part, source, halo, blocks)


def factor(work, nodes, low, high, width):
    half, samples = work.shape[1:]
    octets = half // 8
    row8 = lax.broadcasted_iota(jnp.int32, (nodes, 8, samples), 1)

    def spread_row(value, row):
        return jnp.broadcast_to(value[:, row : row + 1, :], value.shape)

    def spread_column(value, lane):
        flat = value.reshape(nodes * 8, samples)
        return jnp.broadcast_to(flat[:, lane : lane + 1], flat.shape).reshape(value.shape)

    for place in range(low, high):
        base = 8 * place
        head = work[:nodes, base : base + 8, :]
        pivots = None
        for begin in range(0, 8, width):
            rows = range(begin, begin + width)
            columns = {row: spread_column(head, base + row) for row in rows}
            for row in rows:
                pivot = spread_row(columns[row], row)
                pivots = pivot if pivots is None else jnp.where(row8 >= row, pivot, pivots)
                if row == 7:
                    break
                scaled = jnp.where(row8 > row, columns[row] * (1.0 / pivot), 0.0)
                head = head - scaled * spread_row(head, row)
                for later in range(row + 1, begin + width):
                    columns[later] = columns[later] - scaled * spread_row(columns[later], row)
        root = head * lax.rsqrt(pivots)
        work[:nodes, base : base + 8, :] = root
        if place + 1 == octets:
            break
        high_part = root.astype(jnp.bfloat16).astype(jnp.float32)
        rest = root - high_part
        middle = rest.astype(jnp.bfloat16).astype(jnp.float32)
        low_part = rest - middle
        for node in range(nodes):
            h, m, t = high_part[node], middle[node], low_part[node]
            left = jnp.concatenate([h, h, m, m, h, t], axis=0).astype(jnp.bfloat16)
            right = jnp.concatenate([h, m, h, m, t, h], axis=0).astype(jnp.bfloat16)
            update = lax.dot_general(
                left[:, :half],
                right,
                (((0,), (0,)), ((), ())),
                preferred_element_type=jnp.float32,
            )
            work[node, base + 8 :, :] = work[node, base + 8 :, :] - update[base + 8 :, :]


def solved(matrix, right):
    half = right.shape[0]
    blank = jnp.zeros_like(right)
    middle = fine_dot(matrix, jnp.concatenate([blank, right], axis=0))
    return fine_dot(matrix, middle, ((0,), (0,)))[half:]


def packed(gram, moment):
    rows = gram.shape[0] // 2
    half = gram.shape[1] // 2
    lanes = lax.broadcasted_iota(jnp.int32, (rows, 2 * half), 1)
    top = jnp.where(lanes < half, gram[:rows], pltpu.roll(gram[rows:], half, 1))
    return jnp.concatenate([top, moment], axis=0)


def unpacked(value, half):
    rows = half // 2
    lanes = lax.broadcasted_iota(jnp.int32, (half, 2 * half), 1)
    diagonal = lanes - half == lax.broadcasted_iota(jnp.int32, (half, 2 * half), 0)
    gram = jnp.concatenate([value[:rows], pltpu.roll(value[:rows], half, 1)], axis=0)
    return jnp.where(lanes < half, gram, diagonal.astype(jnp.float32))


def tree_kernel(spread, start, moment, work, answers, sums, arrived, sent, landed):
    count, half, samples = start.shape
    depth = count.bit_length() - 1
    me = lax.axis_index(AXIS)
    bits = [lax.rem(lax.div(me, 1 << step), 2) for step in range(spread)]
    partners = [me + (1 - 2 * bit) * (1 << step) for step, bit in enumerate(bits)]
    barrier = pltpu.get_barrier_semaphore()
    for partner in partners:
        pl.semaphore_signal(barrier, inc=1, device_id=(partner,), device_id_type=MESH)

    chunks = sent.shape[1]
    size = sums.shape[1] // chunks

    def exchange(step, chunk):
        part = pl.ds(chunk * size, size)
        return pltpu.make_async_remote_copy(
            src_ref=sums.at[step, part],
            dst_ref=arrived.at[step, part],
            send_sem=sent.at[step, chunk],
            recv_sem=landed.at[step, chunk],
            device_id=(partners[step],),
            device_id_type=MESH,
        )

    grams = {(0, leaf): start[leaf] for leaf in range(count)}
    moments = {(0, leaf): moment[leaf] for leaf in range(count)}
    for height in range(1, depth + 1):
        for node in range(count >> height):
            for table in (grams, moments):
                table[height, node] = (
                    table[height - 1, 2 * node] + table[height - 1, 2 * node + 1]
                )
    sums[0] = packed(grams[depth, 0], moments[depth, 0])
    pl.semaphore_wait(barrier, spread)
    for chunk in range(chunks):
        exchange(0, chunk).start()

    lanes = lax.broadcasted_iota(jnp.int32, (half, samples), 1)
    diagonal = lanes - half == lax.broadcasted_iota(jnp.int32, (half, samples), 0)
    for leaf in range(count):
        work[leaf] = start[leaf]
    place = count
    targets = [(leaf, moments[0, leaf]) for leaf in range(count)]
    for height in range(1, depth + 1):
        targets.append((place, moments[height, 0]))
        for side in range(1 if height == depth else 2):
            work[place] = jnp.where(
                lanes < half, grams[height, side], diagonal.astype(jnp.float32)
            )
            place += 1
    octets = half // 8
    turns = max(spread - 2, 1)
    begin = min(turns, spread - 1)
    for step in range(spread):
        if step < turns:
            factor(work, place, octets * step // turns, octets * (step + 1) // turns, 4)
        if step >= begin:
            some = len(targets) * (step - begin) // (spread - begin)
            more = len(targets) * (step - begin + 1) // (spread - begin)
            for row in range(some, more):
                node, right = targets[row]
                answers[row] = solved(work[node], right)
        for chunk in range(chunks):
            part = pl.ds(chunk * size, size)
            exchange(step, chunk).wait_recv()
            sums[step + 1, part] = sums[step, part] + arrived[step, part]
            if step + 1 < spread:
                exchange(step + 1, chunk).start()
    for step in range(spread):
        for chunk in range(chunks):
            exchange(step, chunk).wait_send()


def tree_call(start, moment, spread):
    count, half, samples = start.shape
    depth = count.bit_length() - 1
    nodes = count + 2 * depth - 1
    rows = half // 2 + half
    vmem = pl.BlockSpec(memory_space=pltpu.VMEM)
    return pl.pallas_call(
        functools.partial(tree_kernel, spread),
        in_specs=[vmem] * 2,
        out_specs=[vmem] * 4,
        out_shape=[
            jax.ShapeDtypeStruct((nodes, half, samples), jnp.float32),
            jax.ShapeDtypeStruct((count + depth, half, samples), jnp.float32),
            jax.ShapeDtypeStruct((spread + 1, rows, samples), jnp.float32),
            jax.ShapeDtypeStruct((spread, rows, samples), jnp.float32),
        ],
        scratch_shapes=[
            pltpu.SemaphoreType.DMA((spread, 3)),
            pltpu.SemaphoreType.DMA((spread, 3)),
        ],
        compiler_params=pltpu.CompilerParams(
            collective_id=1, has_side_effects=True, vmem_limit_bytes=12 * 2**20
        ),
        name="tree",
    )(start, moment)


def out_kernel(
    work, answers, sums, arrived, compact, leaf_out, level_out, tops, leaves, sems
):
    count, rows, samples = compact.shape
    half = answers.shape[1]
    depth = count.bit_length() - 1
    spread = arrived.shape[0]
    me = lax.axis_index(AXIS)
    lanes = lax.broadcasted_iota(jnp.int32, (half, samples), 1)
    triangle = lanes >= lax.broadcasted_iota(jnp.int32, (half, samples), 0)
    corner = triangle & (lanes < half)
    blank = jnp.zeros((half, samples), jnp.float32)

    def sketch(one, two, answer):
        stacked = jnp.concatenate(
            [jnp.where(corner, one, 0.0), jnp.where(corner, two, 0.0)], axis=0
        )
        return fine_dot(stacked, jnp.concatenate([answer, blank], axis=0))

    for step in range(spread):
        tops[2 * step] = unpacked(arrived[step], half)
        tops[2 * step + 1] = unpacked(sums[step + 1], half)
    octets = half // 8
    copies = []
    for turn in range(octets):
        factor(tops, 2 * spread, turn, turn + 1, 8)
        first, last = count * turn // octets, count * (turn + 1) // octets
        for leaf in range(first, last):
            answer = answers[leaf]
            high = answer.astype(jnp.bfloat16)
            low = (answer - high.astype(jnp.float32)).astype(jnp.bfloat16)
            pair = jnp.concatenate([high, low], axis=1)
            both = jnp.dot(
                compact[leaf],
                jnp.concatenate([pair, pair], axis=0),
                preferred_element_type=jnp.float32,
            )
            leaves[leaf] = (both[:, :samples] + both[:, samples:]).astype(leaves.dtype)
        if last > first:
            part = pl.ds(first, last - first)
            copy = pltpu.make_async_copy(leaves.at[part], leaf_out.at[part], sems.at[turn])
            copy.start()
            copies.append(copy)
    for height in range(1, depth + 1):
        first = 0 if height == 1 else count + 2 * (height - 2)
        level_out[0, height - 1] = sketch(
            work[first], work[first + 1], answers[count + height - 1]
        ).astype(level_out.dtype)
    for step in range(spread):
        mine = work[count + 2 * (depth - 1)] if step == 0 else tops[2 * step - 1]
        other = tops[2 * step]
        odd = lax.rem(lax.div(me, 1 << step), 2) == 1
        answer = solved(tops[2 * step + 1], sums[step + 1, half // 2 :, :])
        level_out[0, depth + step] = sketch(
            jnp.where(odd, other, mine), jnp.where(odd, mine, other), answer
        ).astype(level_out.dtype)
    for copy in copies:
        copy.wait()


def out_call(work, answers, sums, arrived, compact):
    count, rows, samples = compact.shape
    half = answers.shape[1]
    spread = arrived.shape[0]
    depth = count.bit_length() - 1
    vmem = pl.BlockSpec(memory_space=pltpu.VMEM)
    return pl.pallas_call(
        out_kernel,
        in_specs=[vmem] * 5,
        out_specs=[pl.BlockSpec(memory_space=pl.ANY), vmem],
        out_shape=[
            jax.ShapeDtypeStruct((count, rows, samples), jnp.bfloat16),
            jax.ShapeDtypeStruct((1, depth + spread, samples, samples), jnp.bfloat16),
        ],
        scratch_shapes=[
            pltpu.VMEM((2 * spread, half, samples), jnp.float32),
            pltpu.VMEM((count, rows, samples), jnp.bfloat16),
            pltpu.SemaphoreType.DMA((half // 8,)),
        ],
        compiler_params=pltpu.CompilerParams(vmem_limit_bytes=12 * 2**20),
        name="out",
    )(work, answers, sums, arrived, compact)


def per_device(random_block, sample_block, near_blocks, near_index, near_count):
    spread = lax.axis_size(AXIS).bit_length() - 1
    index = near_index.T
    fixed = [
        pltpu.with_memory_space_constraint(value, pltpu.HBM)
        for value in (index, near_count, random_block, near_blocks, sample_block)
    ]
    part, halo, held = halo_call(*fixed)
    start, moment, compact = gram_call(
        index, near_count, part, random_block, halo, held
    )
    work, answers, sums, arrived = tree_call(start, moment, spread)
    return tuple(out_call(work, answers, sums, arrived, compact))


def solution(mesh):
    return jax.shard_map(
        per_device,
        mesh=mesh,
        in_specs=(
            P(AXIS, None, None),
            P(AXIS, None, None),
            P(AXIS, None, None, None),
            P(AXIS, None),
            P(AXIS),
        ),
        out_specs=(P(AXIS, None, None), P(AXIS, None, None, None)),
        check_vma=False,
    )
```
